512 devices in a mesh: grp: 8 (over y), sp: 64 (over x, z, core).
Axes of the slice: x: 4, y: 8, z: 8, core: 2. Of those that a mesh axis runs over, the one named last changes fastest.
Arguments:
- snapshots: float32 [3, 8192, 24576], P(None, 'grp', 'sp'), may hold values from -12 to 12
- kept_bins: int32 [64], replicated, may hold values from 1 to 255, as said below
- weights: float32 [24576], P('sp'), may hold values from 0.1 to 80
Outputs:
- mode_fields: float32 [2, 64, 4, 3, 24576], P(None, 'grp', None, None, 'sp')
- energies: float32 [64, 4], P('grp')
The draws below stay inside these ranges and needn't reach their ends.
Inputs may be any that keep to these rules, and one draw needn't show every extreme that they name: `kept_bins`: 64 distinct bins in increasing order; both 1 and 255 are among them.
All inputs are finite; a program needn't handle non-finite values.
Results may differ from the reference program's by a relative error of at most 0.0003.
Values sent between devices are 32-bit elements; how exact they have to be, the bound alone decides.
A program may use at most 64 MiB of HBM per device.

```python
import math
import jax
import jax.numpy as jnp
from jax import lax

L = 512
HOP = 256
NF = 64
MODES = 4
ITERS = 3
NBLK = 32
NT = 8192
P_SIZE = 24576


def draw_snapshots(key, part):
    folded = jax.random.fold_in(key, 11)
    subkeys = jax.random.split(folded, 4)
    noise_part = jax.random.normal(subkeys[0], (3, NT, P_SIZE), jnp.float32)
    region = jnp.arange(P_SIZE, dtype=jnp.int32) * 16 // P_SIZE
    envelope = jnp.exp(jax.random.uniform(subkeys[1], (4, 16), jnp.float32, -1.0, 1.0))[:, region]
    strength = jnp.array([0.6, 0.4, 0.25, 0.15], jnp.float32)
    shapes = jax.random.normal(subkeys[2], (4, 3, P_SIZE), jnp.float32) * jnp.sqrt(strength)[:, None, None] * envelope[:, None, :]
    signal = jax.random.normal(subkeys[3], (4, NT), jnp.float32)
    velocity = noise_part
    for component in range(4):
        velocity = velocity + shapes[component][:, None, :] * signal[component][None, :, None]
    return jnp.clip(velocity, -12.0, 12.0)


def draw_kept_bins(key, part):
    folded = jax.random.fold_in(key, 37)
    inner = jax.random.permutation(folded, L // 2 - 3).astype(jnp.int32) + 2
    picked = jnp.concatenate([jnp.array([1, L // 2 - 1], jnp.int32), inner[:NF - 2]])
    return jnp.sort(picked).astype(jnp.int32)


def draw_weights(key, part):
    folded = jax.random.fold_in(key, 23)
    subkeys = jax.random.split(folded, 2)
    position = jnp.arange(P_SIZE, dtype=jnp.float32) / P_SIZE
    ramp = jnp.exp(math.log(3.0) * position)
    region = jnp.arange(P_SIZE, dtype=jnp.int32) * 16 // P_SIZE
    regional = jnp.exp(jax.random.uniform(subkeys[0], (16,), jnp.float32, math.log(0.25), math.log(4.0)))[region]
    pointwise = jnp.exp(jax.random.uniform(subkeys[1], (P_SIZE,), jnp.float32, math.log(0.5), math.log(2.0)))
    return ramp * regional * pointwise


def setup_inputs(seed: int = 0) -> dict:
    key_of = jax.random.split(jax.random.key(seed), 4)
    return {
        "snapshots": draw_snapshots(jax.random.fold_in(key_of[3], 71), 0),
        "kept_bins": draw_kept_bins(jax.random.fold_in(key_of[3], 71), 0),
        "weights": draw_weights(jax.random.fold_in(key_of[3], 71), 0),
    }


precise = lax.Precision.HIGHEST

def orthonormalize(w_real, w_imag):
    basis_re = []
    basis_im = []
    lengths = []
    for column in range(w_real.shape[-1]):
        orig_re = w_real[..., column]
        orig_im = w_imag[..., column]
        left_re = orig_re
        left_im = orig_im
        for earlier in range(column):
            prev_re = basis_re[earlier]
            prev_im = basis_im[earlier]
            coef_re = lax.optimization_barrier(jnp.sum(prev_re * orig_re + prev_im * orig_im, axis=-1, keepdims=True))
            coef_im = lax.optimization_barrier(jnp.sum(prev_re * orig_im - prev_im * orig_re, axis=-1, keepdims=True))
            left_re = left_re - (coef_re * prev_re - coef_im * prev_im)
            left_im = left_im - (coef_re * prev_im + coef_im * prev_re)
        length = jnp.sqrt(lax.optimization_barrier(jnp.sum(left_re * left_re + left_im * left_im, axis=-1)) + 1e-06)
        basis_re.append(left_re / length[..., None])
        basis_im.append(left_im / length[..., None])
        lengths.append(length)
    return (jnp.stack(basis_re, -1), jnp.stack(basis_im, -1), jnp.stack(lengths, -1))

def apply_gram(gram_re, gram_im, v_real, v_imag):
    pattern = 'fbd,fdm->fbm'
    out_re = jnp.einsum(pattern, gram_re, v_real, precision=precise) - jnp.einsum(pattern, gram_im, v_imag, precision=precise)
    out_im = jnp.einsum(pattern, gram_re, v_imag, precision=precise) + jnp.einsum(pattern, gram_im, v_real, precision=precise)
    return (out_re, out_im)

def subspace(apply_fn, freq_count, block_count, mode_count):
    identity_cols = jnp.eye(block_count, mode_count, dtype=jnp.float32)
    v_real = jnp.broadcast_to(identity_cols, (freq_count, block_count, mode_count))
    v_imag = jnp.zeros((freq_count, block_count, mode_count), jnp.float32)
    lengths = jnp.zeros((freq_count, mode_count), jnp.float32)
    for sweep_step in range(ITERS):
        w_real, w_imag = apply_fn(v_real, v_imag)
        v_real, v_imag, lengths = orthonormalize(w_real, w_imag)
    return (v_real, v_imag, lengths)

def local_gram(x_real, x_imag, point_wts, norm_factor):
    y_real = x_real * point_wts
    y_imag = x_imag * point_wts
    pattern = 'bfcp,dfcp->fbd'
    g_re = (jnp.einsum(pattern, y_real, x_real, precision=precise) + jnp.einsum(pattern, y_imag, x_imag, precision=precise)) * norm_factor
    g_im = (jnp.einsum(pattern, y_real, x_imag, precision=precise) - jnp.einsum(pattern, y_imag, x_real, precision=precise)) * norm_factor
    return (g_re, g_im)

def form_modes(x_real, x_imag, v_real, v_imag, lengths, block_count):
    pattern = 'bfcp,fbm->fmcp'
    m_re = jnp.einsum(pattern, x_real, v_real, precision=precise) - jnp.einsum(pattern, x_imag, v_imag, precision=precise)
    m_im = jnp.einsum(pattern, x_real, v_imag, precision=precise) + jnp.einsum(pattern, x_imag, v_real, precision=precise)
    factor = (1.0 / jnp.sqrt(block_count * lengths))[:, :, None, None]
    return jnp.stack([m_re * factor, m_im * factor])

def reference(snapshots, kept_bins, weights):
    total_time = snapshots.shape[1]
    total_points = snapshots.shape[2]
    offsets = jnp.arange(L, dtype=jnp.int32)
    window = (0.5 - 0.5 * jnp.cos(offsets.astype(jnp.float32) * (2.0 * math.pi / L))) / math.sqrt(3.0 * L / 8.0)

    def spectrum(block_id):
        positions = ((block_id * HOP + offsets) % total_time).astype(jnp.int32)
        segment_in = jnp.take(snapshots, positions, axis=1) * window[None, :, None]
        transformed = jnp.fft.rfft(segment_in, axis=1)
        chosen = jnp.take(transformed, kept_bins, axis=1)
        return jnp.stack([jnp.real(chosen), jnp.imag(chosen)]).astype(jnp.float32)
    spectra = lax.map(spectrum, jnp.arange(NBLK, dtype=jnp.int32))
    x_real = jnp.transpose(spectra[:, 0], (0, 2, 1, 3))
    x_imag = jnp.transpose(spectra[:, 1], (0, 2, 1, 3))
    norm_factor = 1.0 / (3.0 * total_points)
    g_re, g_im = local_gram(x_real, x_imag, weights, norm_factor)

    def apply_fn(v_real, v_imag):
        return apply_gram(g_re, g_im, v_real, v_imag)
    v_real, v_imag, lengths = subspace(apply_fn, NF, NBLK, MODES)
    mode_fields = form_modes(x_real, x_imag, v_real, v_imag, lengths, NBLK)
    return (mode_fields, lengths)
```

```python
import functools
import math

import jax
import jax.numpy as jnp
from jax import lax
from jax.experimental import pallas as pl
from jax.experimental.pallas import tpu as pltpu
from jax.sharding import PartitionSpec as P

L = 512
HOP = 256
MODES = 4
ITERS = 3
GRP = 8
FPG = 8
RED = 8
ZS = 8
CORES = 2
NB = 4
NBLK = GRP * NB
MESH = pl.DeviceIdType.MESH


def cos_sin(phase):
    quarter = (phase + 64) >> 7
    rest = (phase - (quarter << 7)).astype(jnp.float32) * (2.0 * math.pi / L)
    sq = rest * rest
    sin = rest * (1.0 + sq * (-1.0 / 6 + sq * (1.0 / 120 + sq * (-1.0 / 5040 + sq * (1.0 / 362880)))))
    cos = 1.0 + sq * (-0.5 + sq * (1.0 / 24 + sq * (-1.0 / 720 + sq * (1.0 / 40320 - sq * (1.0 / 3628800)))))
    quarter = quarter & 3
    odd = (quarter & 1) == 1
    cos_q = jnp.where(odd, sin, cos)
    sin_q = jnp.where(odd, cos, sin)
    cos_q = jnp.where((quarter == 1) | (quarter == 2), -cos_q, cos_q)
    sin_q = jnp.where(quarter >= 2, -sin_q, sin_q)
    return cos_q, sin_q


def split(x):
    high = x.astype(jnp.bfloat16)
    low = (x - high.astype(jnp.float32)).astype(jnp.bfloat16)
    return high, low


def fdot(a, b):
    return jnp.dot(a, b, preferred_element_type=jnp.float32)


def make_tables(bins_ref, tab_hi, tab_lo):
    shape = (FPG, HOP)
    row = lax.broadcasted_iota(jnp.int32, shape, 0)
    time = lax.broadcasted_iota(jnp.int32, shape, 1)
    scale = 1.0 / math.sqrt(3.0 * L / 8.0)
    window = (0.5 - 0.5 * cos_sin(time)[0]) * scale
    second = scale - window
    for group in range(GRP):
        bins = jnp.full(shape, bins_ref[group * FPG], jnp.int32)
        for f in range(1, FPG):
            bins = jnp.where(row == f, bins_ref[group * FPG + f], bins)
        cos, sin = cos_sin((bins * time) & (L - 1))
        signed = jnp.where((bins & 1) == 1, -second, second)
        base = group * 2 * FPG
        for part, wave in ((0, cos), (1, -sin)):
            rows = pl.ds(base + part * FPG, FPG)
            for half, win in ((0, window), (1, signed)):
                high, low = split(wave * win)
                tab_hi[rows, half * HOP : (half + 1) * HOP] = high
                tab_lo[rows, half * HOP : (half + 1) * HOP] = low


def orthonormalize(w):
    lane = lax.broadcasted_iota(jnp.int32, w.shape, 1)
    lane_row = lax.broadcasted_iota(jnp.int32, (1, w.shape[1]), 1)
    w_re, w_im = w[:NBLK], w[NBLK:]
    left = w
    basis = jnp.zeros_like(w)
    lengths = jnp.ones((1, w.shape[1]), jnp.float32)
    for m in range(MODES):
        length = jnp.sqrt(jnp.sum(left * left, axis=0, keepdims=True) + 1e-06)
        unit = left / length
        basis = jnp.where(lane == m, unit, basis)
        lengths = jnp.where(lane_row == m, length, lengths)
        if m < MODES - 1:
            q = jnp.broadcast_to(unit[:, m : m + 1], w.shape)
            q_re, q_im = q[:NBLK], q[NBLK:]
            coef_re = jnp.sum(q_re * w_re + q_im * w_im, axis=0, keepdims=True)
            coef_im = jnp.sum(q_re * w_im - q_im * w_re, axis=0, keepdims=True)
            left = left - jnp.concatenate(
                [coef_re * q_re - coef_im * q_im, coef_re * q_im + coef_im * q_re], axis=0
            )
    return basis, lengths


def kernel(
    norm,
    bins_ref,
    wts_ref,
    snap_ref,
    modes_ref,
    en_ref,
    data,
    d_hi,
    d_lo,
    tab_hi,
    tab_lo,
    send,
    recv,
    hsend,
    hrecv,
    gram,
    gsend,
    rrecv,
    zpart,
    zrecv,
    vsend,
    vrecv,
    coef,
    in_sem,
    own_sem,
    h_ssem,
    h_rsem,
    a_ssem,
    a_rsem,
    r_ssem,
    r_rsem,
    z_ssem,
    z_rsem,
    v_ssem,
    v_rsem,
):
    comps = data.shape[0]
    points = data.shape[2]
    grp = lax.axis_index("grp")
    sp = lax.axis_index("sp")
    core = sp % CORES
    z = (sp // CORES) % ZS
    x = sp // (CORES * ZS)
    red = x * CORES + core

    def grp_peer(off):
        return (grp + off) % GRP, sp

    def red_peer(off):
        other = (red + off) % RED
        return grp, ((other // CORES) * ZS + z) * CORES + other % CORES

    def z_peer(off):
        return grp, (x * ZS + (z + off) % ZS) * CORES + core

    barrier = pltpu.get_barrier_semaphore()
    for peer in (grp_peer, red_peer, z_peer):
        for off in range(1, 8):
            pl.semaphore_signal(barrier, inc=1, device_id=peer(off), device_id_type=MESH)

    def load(c, h):
        rows = pl.ds(h * HOP, HOP)
        return pltpu.make_async_copy(snap_ref.at[c, rows], data.at[c, rows], in_sem.at[h, c])

    for h in range(NB):
        for c in range(comps):
            load(c, h).start()

    make_tables(bins_ref, tab_hi, tab_lo)

    def convert(c, h):
        load(c, h).wait()
        rows = pl.ds(h * HOP, HOP)
        high, low = split(data[c, rows])
        d_hi[c, rows] = high
        d_lo[c, rows] = low

    def transform(c, h_first, cols):
        rows = pl.ds(h_first * HOP, cols.stop - cols.start)
        high = d_hi[c, rows]
        t_hi = tab_hi[:, cols]
        return fdot(t_hi, high) + (fdot(tab_lo[:, cols], high) + fdot(t_hi, d_lo[c, rows]))

    def halo_copy(c):
        return pltpu.make_async_remote_copy(
            hsend.at[c], hrecv.at[c], h_ssem.at[c], h_rsem.at[c],
            device_id=grp_peer(GRP - 1), device_id_type=MESH,
        )

    tiles = points // 128
    comp_rows = tiles * 2 * FPG
    blk_rows = comps * comp_rows

    def rows_at(block, c, count):
        start = pl.multiple_of(block * blk_rows + c * comp_rows, 2 * FPG)
        return pl.ds(start, count * comp_rows)

    def block_copy(off, h):
        to = (grp + off) % GRP
        return pltpu.make_async_remote_copy(
            send.at[rows_at(to * NB + h, 0, comps)],
            recv.at[rows_at(grp * NB + h, 0, comps)],
            a_ssem.at[h, off], a_rsem.at[h, off],
            device_id=grp_peer(off), device_id_type=MESH,
        )

    def last_copy(off, c):
        to = (grp + off) % GRP
        return pltpu.make_async_remote_copy(
            send.at[rows_at(to * NB + NB - 1, c, 1)],
            recv.at[rows_at(grp * NB + NB - 1, c, 1)],
            a_ssem.at[NB - 1 + c, off], a_rsem.at[NB - 1 + c, off],
            device_id=grp_peer(off), device_id_type=MESH,
        )

    def own_copy(h):
        rows = rows_at(grp * NB + h, 0, comps)
        return pltpu.make_async_copy(send.at[rows], recv.at[rows], own_sem.at[h])

    def own_last(c):
        rows = rows_at(grp * NB + NB - 1, c, 1)
        return pltpu.make_async_copy(send.at[rows], recv.at[rows], own_sem.at[NB - 1 + c])

    def put(c, h, out):
        for to in range(GRP):
            for tile in range(tiles):
                rows = pl.ds((to * NB + h) * blk_rows + c * comp_rows + tile * 2 * FPG, 2 * FPG)
                send[rows, :] = out[to * 2 * FPG : (to + 1) * 2 * FPG, tile * 128 : (tile + 1) * 128]

    order = (4, 3, 5, 2, 6, 1, 7)
    both = slice(0, 2 * HOP)

    for c in range(comps):
        convert(c, 0)
        hsend[c] = transform(c, 0, slice(HOP, 2 * HOP))
        if c == 0:
            pl.semaphore_wait(barrier, 21)
        halo_copy(c).start()

    for h in range(NB - 1):
        for c in range(comps):
            convert(c, h + 1)
            put(c, h, transform(c, h, both))
        for off in order:
            block_copy(off, h).start()
        own_copy(h).start()

    for c in range(comps):
        out = transform(c, NB - 1, slice(0, HOP))
        halo_copy(c).wait_recv()
        put(c, NB - 1, out + hrecv[c])
        for off in order:
            last_copy(off, c).start()
        own_last(c).start()

    scale = jnp.sqrt(wts_ref[...] * norm)
    for h in range(NB - 1):
        own_copy(h).wait()
        for off in order:
            block_copy(off, h).wait_recv()

    def gather(c, row):
        starts = [c * comp_rows + tile * 2 * FPG + row for tile in range(tiles)]
        return jnp.concatenate(
            [recv[pl.ds(start, NBLK, stride=blk_rows), :] for start in starts], axis=1
        )

    for c in range(comps):
        own_last(c).wait()
        for off in order:
            last_copy(off, c).wait_recv()
        for f in range(FPG):
            re = gather(c, f)
            im = gather(c, FPG + f)
            both_parts = jnp.concatenate([re, im], axis=0) * scale
            high, low = split(both_parts)
            stack = jnp.concatenate([high, low], axis=0)
            prod = lax.dot_general(
                stack, stack, (((1,), (1,)), ((), ())), preferred_element_type=jnp.float32
            )
            half = prod[: 2 * NBLK] + prod[2 * NBLK :]
            gram[f] = half if c == 0 else gram[f] + half

    lane16 = lax.broadcasted_iota(jnp.int32, (NBLK // 2, 128), 1)
    lane32 = lax.broadcasted_iota(jnp.int32, (NBLK, 128), 1)
    for f in range(FPG):
        whole = gram[f]
        whole = whole + pltpu.roll(whole, 64, 1)
        low_rows = pltpu.roll(whole[NBLK:], 32, 1)
        joined = whole[:NBLK] + jnp.where((lane32 & 32) == 0, low_rows, -low_rows)
        gsend[f] = jnp.where(lane16 < 64, joined[: NBLK // 2], joined[NBLK // 2 :])

    def red_copy(off):
        return pltpu.make_async_remote_copy(
            gsend.at[(red + off) % RED], rrecv.at[red], r_ssem.at[off], r_rsem.at[off],
            device_id=red_peer(off), device_id_type=MESH,
        )

    for off in range(1, RED):
        red_copy(off).start()
    part = gsend[red]
    for off in range(1, RED):
        red_copy(off).wait_recv()
        part = part + rrecv[(red + RED - off) % RED]
    zpart[...] = part

    def z_copy(off):
        return pltpu.make_async_remote_copy(
            zpart, zrecv.at[z], z_ssem.at[off], z_rsem.at[off],
            device_id=z_peer(off), device_id_type=MESH,
        )

    for off in range(1, ZS):
        z_copy(off).start()
    zrecv[z] = part
    for off in range(1, ZS):
        z_copy(off).wait_recv()
    total = zrecv[0]
    for i in range(1, ZS):
        total = total + zrecv[i]

    rows_g = jnp.concatenate([total, pltpu.roll(total, 64, 1)], axis=0)
    upper = jnp.where(lane32 < 32, rows_g, jnp.where(lane32 < 64, -rows_g, 0.0))
    lower = jnp.where(
        lane32 < 32,
        pltpu.roll(rows_g, 96, 1),
        jnp.where(lane32 < 64, pltpu.roll(rows_g, 32, 1), 0.0),
    )
    embed = jnp.concatenate([upper, lower], axis=0)
    w = embed
    for step in range(ITERS):
        basis, lengths = orthonormalize(w)
        if step < ITERS - 1:
            padded = jnp.concatenate([basis, jnp.zeros_like(basis)], axis=0)
            w = jnp.dot(
                embed, padded, precision=lax.Precision.HIGHEST, preferred_element_type=jnp.float32
            )
    scaled = basis * (1.0 / jnp.sqrt(NBLK * lengths))
    column = jnp.concatenate([scaled, jnp.broadcast_to(lengths, scaled.shape)], axis=0)
    vsend[...] = jnp.transpose(column)[:8]

    def v_copy(off):
        return pltpu.make_async_remote_copy(
            vsend, vrecv.at[red], v_ssem.at[off], v_rsem.at[off],
            device_id=red_peer(off), device_id_type=MESH,
        )

    for off in range(1, RED):
        v_copy(off).start()
    vrecv[red] = vsend[...]
    for off in range(1, RED):
        v_copy(off).wait_recv()

    lane8 = lax.broadcasted_iota(jnp.int32, (FPG, 128), 1)
    energies = jnp.zeros((FPG, 128), jnp.float32)
    for m in range(MODES):
        cols = vrecv[:, m, :]
        for b in range(2 * NBLK):
            coef[b, m] = jnp.broadcast_to(cols[:, b : b + 1], (FPG, 128))
        energies = jnp.where(
            lane8 == m, jnp.broadcast_to(cols[:, 2 * NBLK : 2 * NBLK + 1], (FPG, 128)), energies
        )
    en_ref[...] = energies[:, :MODES]

    def mode_tile(i, carry):
        c = i // tiles
        lanes = pl.ds(pl.multiple_of((i % tiles) * 128, 128), 128)
        acc_re = [jnp.zeros((FPG, 128), jnp.float32)] * MODES
        acc_im = [jnp.zeros((FPG, 128), jnp.float32)] * MODES
        for b in range(NBLK):
            start = pl.multiple_of(b * blk_rows + i * 2 * FPG, 2 * FPG)
            x_re = recv[pl.ds(start, FPG), :]
            x_im = recv[pl.ds(start + FPG, FPG), :]
            for m in range(MODES):
                v_re = coef[b, m]
                v_im = coef[NBLK + b, m]
                acc_re[m] = acc_re[m] + (x_re * v_re - x_im * v_im)
                acc_im[m] = acc_im[m] + (x_re * v_im + x_im * v_re)
        for m in range(MODES):
            modes_ref[0, m, c, :, lanes] = acc_re[m]
            modes_ref[1, m, c, :, lanes] = acc_im[m]
        return carry

    lax.fori_loop(0, comps * tiles, mode_tile, 0)

    for c in range(comps):
        halo_copy(c).wait_send()
    for off in order:
        for h in range(NB - 1):
            block_copy(off, h).wait_send()
        for c in range(comps):
            last_copy(off, c).wait_send()
    for off in range(1, 8):
        red_copy(off).wait_send()
        z_copy(off).wait_send()
        v_copy(off).wait_send()


def shards(snapshots, kept_bins, weights):
    comps, times, points = snapshots.shape
    norm = 1.0 / (comps * points * lax.axis_size("sp"))
    f32, bf16 = jnp.float32, jnp.bfloat16
    dma = pltpu.SemaphoreType.DMA
    modes, energies = pl.pallas_call(
        functools.partial(kernel, norm),
        out_shape=(
            jax.ShapeDtypeStruct((2, MODES, comps, FPG, points), f32),
            jax.ShapeDtypeStruct((FPG, MODES), f32),
        ),
        in_specs=[
            pl.BlockSpec(memory_space=pltpu.SMEM),
            pl.BlockSpec(memory_space=pltpu.VMEM),
            pl.BlockSpec(memory_space=pl.ANY),
        ],
        out_specs=(
            pl.BlockSpec(memory_space=pltpu.VMEM),
            pl.BlockSpec(memory_space=pltpu.VMEM),
        ),
        scratch_shapes=[
            pltpu.VMEM((comps, times, points), f32),
            pltpu.VMEM((comps, times, points), bf16),
            pltpu.VMEM((comps, times, points), bf16),
            pltpu.VMEM((2 * FPG * GRP, L), bf16),
            pltpu.VMEM((2 * FPG * GRP, L), bf16),
            pltpu.VMEM((NBLK * 2 * FPG * comps * points // 128, 128), f32),
            pltpu.VMEM((NBLK * 2 * FPG * comps * points // 128, 128), f32),
            pltpu.VMEM((comps, 2 * FPG * GRP, points), f32),
            pltpu.VMEM((comps, 2 * FPG * GRP, points), f32),
            pltpu.VMEM((FPG, 2 * NBLK, 128), f32),
            pltpu.VMEM((FPG, NBLK // 2, 128), f32),
            pltpu.VMEM((RED, NBLK // 2, 128), f32),
            pltpu.VMEM((NBLK // 2, 128), f32),
            pltpu.VMEM((ZS, NBLK // 2, 128), f32),
            pltpu.VMEM((8, 128), f32),
            pltpu.VMEM((RED, 8, 128), f32),
            pltpu.VMEM((2 * NBLK, MODES, FPG, 128), f32),
            dma((NB, comps)),
            dma((NB - 1 + comps,)),
            dma((comps,)),
            dma((comps,)),
            dma((NB - 1 + comps, GRP)),
            dma((NB - 1 + comps, GRP)),
            dma((RED,)),
            dma((RED,)),
            dma((ZS,)),
            dma((ZS,)),
            dma((RED,)),
            dma((RED,)),
        ],
        compiler_params=pltpu.CompilerParams(
            collective_id=0, has_side_effects=True, vmem_limit_bytes=48 << 20
        ),
    )(kept_bins, weights.reshape(1, points), snapshots)
    return (jnp.transpose(modes, (0, 3, 1, 2, 4)), energies)


def solution(mesh):
    in_specs = (P(None, "grp", "sp"), P(), P("sp"))
    out_specs = (P(None, "grp", None, None, "sp"), P("grp", None))
    return jax.shard_map(shards, mesh=mesh, in_specs=in_specs, out_specs=out_specs, check_vma=False)
```

```python
import functools
import math

import jax
import jax.numpy as jnp
from jax import lax
from jax.experimental import pallas as pl
from jax.experimental.pallas import tpu as pltpu
from jax.sharding import PartitionSpec as P

L = 512
HOP = 256
MODES = 4
ITERS = 3
GRP = 8
FPG = 8
RED = 8
ZS = 8
CORES = 2
NB = 4
NBLK = GRP * NB
MESH = pl.DeviceIdType.MESH


def cos_sin(phase):
    quarter = (phase + 64) >> 7
    rest = (phase - (quarter << 7)).astype(jnp.float32) * (2.0 * math.pi / L)
    sq = rest * rest
    sin = rest * (1.0 + sq * (-1.0 / 6 + sq * (1.0 / 120 + sq * (-1.0 / 5040 + sq * (1.0 / 362880)))))
    cos = 1.0 + sq * (-0.5 + sq * (1.0 / 24 + sq * (-1.0 / 720 + sq * (1.0 / 40320 - sq * (1.0 / 3628800)))))
    quarter = quarter & 3
    odd = (quarter & 1) == 1
    cos_q = jnp.where(odd, sin, cos)
    sin_q = jnp.where(odd, cos, sin)
    cos_q = jnp.where((quarter == 1) | (quarter == 2), -cos_q, cos_q)
    sin_q = jnp.where(quarter >= 2, -sin_q, sin_q)
    return cos_q, sin_q


def split(x):
    high = x.astype(jnp.bfloat16)
    low = (x - high.astype(jnp.float32)).astype(jnp.bfloat16)
    return high, low


def fdot(a, b):
    return jnp.dot(a, b, preferred_element_type=jnp.float32)


def make_tables(first_group, bins_ref, tab_hi, tab_lo):
    shape = (FPG, HOP)
    row = lax.broadcasted_iota(jnp.int32, shape, 0)
    time = lax.broadcasted_iota(jnp.int32, shape, 1)
    scale = 1.0 / math.sqrt(3.0 * L / 8.0)
    window = (0.5 - 0.5 * cos_sin(time)[0]) * scale
    second = scale - window
    for off in range(GRP):
        group = (first_group + off) % GRP
        bins = jnp.full(shape, bins_ref[group * FPG], jnp.int32)
        for f in range(1, FPG):
            bins = jnp.where(row == f, bins_ref[group * FPG + f], bins)
        cos, sin = cos_sin((bins * time) & (L - 1))
        signed = jnp.where((bins & 1) == 1, -second, second)
        for half, win in ((0, window), (1, signed)):
            high, low = split(jnp.concatenate([cos * win, -sin * win], axis=0))
            rows = pl.ds(off * 2 * FPG, 2 * FPG)
            tab_hi[rows, half * HOP : (half + 1) * HOP] = high
            tab_lo[rows, half * HOP : (half + 1) * HOP] = low


def orthonormalize(w):
    lane = lax.broadcasted_iota(jnp.int32, w.shape, 1)
    lane_row = lax.broadcasted_iota(jnp.int32, (1, w.shape[1]), 1)
    w_re, w_im = w[:NBLK], w[NBLK:]
    left = w
    basis = jnp.zeros_like(w)
    lengths = jnp.ones((1, w.shape[1]), jnp.float32)
    for m in range(MODES):
        length = jnp.sqrt(jnp.sum(left * left, axis=0, keepdims=True) + 1e-06)
        unit = left / length
        basis = jnp.where(lane == m, unit, basis)
        lengths = jnp.where(lane_row == m, length, lengths)
        if m < MODES - 1:
            q = jnp.broadcast_to(unit[:, m : m + 1], w.shape)
            q_re, q_im = q[:NBLK], q[NBLK:]
            coef_re = jnp.sum(q_re * w_re + q_im * w_im, axis=0, keepdims=True)
            coef_im = jnp.sum(q_re * w_im - q_im * w_re, axis=0, keepdims=True)
            left = left - jnp.concatenate(
                [coef_re * q_re - coef_im * q_im, coef_re * q_im + coef_im * q_re], axis=0
            )
    return basis, lengths


def kernel(
    norm,
    bins_hbm,
    wts_hbm,
    snap_ref,
    modes_ref,
    en_ref,
    bins_ref,
    wts_ref,
    data,
    d_hi,
    d_lo,
    tab_hi,
    tab_lo,
    send,
    recv,
    a_send,
    d_send,
    a_keep,
    d_keep,
    a_recv,
    d_recv,
    gram,
    zs,
    gsend,
    rrecv,
    zpart,
    zrecv,
    vsend,
    vrecv,
    in_sem,
    arg_sem,
    own_sem,
    h_ssem,
    h_rsem,
    a_ssem,
    a_rsem,
    r_ssem,
    r_rsem,
    z_ssem,
    z_rsem,
    v_ssem,
    v_rsem,
):
    comps = data.shape[0]
    points = data.shape[2]
    tiles = points // 128
    comp_rows = tiles * 2 * FPG
    blk_rows = comps * comp_rows
    half_rows = GRP * FPG
    grp = lax.axis_index("grp")
    sp = lax.axis_index("sp")
    core = sp % CORES
    z = (sp // CORES) % ZS
    x = sp // (CORES * ZS)
    red = x * CORES + core

    def grp_peer(off):
        return (grp + off) % GRP, sp

    def red_peer(off):
        other = (red + off) % RED
        return grp, ((other // CORES) * ZS + z) * CORES + other % CORES

    def z_peer(off):
        return grp, (x * ZS + (z + off) % ZS) * CORES + core

    bins_copy = pltpu.make_async_copy(bins_hbm, bins_ref, arg_sem.at[0])
    wts_copy = pltpu.make_async_copy(wts_hbm, wts_ref, arg_sem.at[1])
    bins_copy.start()

    def load(c, h):
        rows = pl.ds(h * HOP, HOP)
        return pltpu.make_async_copy(snap_ref.at[c, rows], data.at[c, rows], in_sem.at[h, c])

    for h in (0, NB - 1):
        for c in range(comps):
            load(c, h).start()
    barrier = pltpu.get_barrier_semaphore()
    for off in (4, 3, 5, 2, 6, 1, 7):
        for peer in (grp_peer, z_peer, red_peer):
            pl.semaphore_signal(barrier, inc=1, device_id=peer(off), device_id_type=MESH)
    for h in range(1, NB - 1):
        for c in range(comps):
            load(c, h).start()
    wts_copy.start()

    bins_copy.wait()
    make_tables(grp, bins_ref, tab_hi, tab_lo)

    def convert(c, h):
        load(c, h).wait()
        rows = pl.ds(h * HOP, HOP)
        high, low = split(data[c, rows])
        d_hi[c, rows] = high
        d_lo[c, rows] = low

    def transform(c, h_first, cols):
        rows = pl.ds(h_first * HOP, cols.stop - cols.start)
        high = d_hi[c, rows]
        t_hi = tab_hi[:, cols]
        return fdot(t_hi, high) + (fdot(tab_lo[:, cols], high) + fdot(t_hi, d_lo[c, rows]))

    def a_copy(c):
        return pltpu.make_async_remote_copy(
            a_send.at[c], a_recv.at[c], h_ssem.at[0, c], h_rsem.at[0, c],
            device_id=grp_peer(1), device_id_type=MESH,
        )

    def d_copy(c):
        return pltpu.make_async_remote_copy(
            d_send.at[c], d_recv.at[c], h_ssem.at[1, c], h_rsem.at[1, c],
            device_id=grp_peer(GRP - 1), device_id_type=MESH,
        )

    def rows_at(block, c, count):
        start = pl.multiple_of(block * blk_rows + c * comp_rows, 2 * FPG)
        return pl.ds(start, count * comp_rows)

    def block_copy(off, h):
        return pltpu.make_async_remote_copy(
            send.at[rows_at(off * NB + h, 0, comps)],
            recv.at[rows_at(grp * NB + h, 0, comps)],
            a_ssem.at[h, off], a_rsem.at[h, off],
            device_id=grp_peer(off), device_id_type=MESH,
        )

    left_block = (grp * NB + NBLK - 1) % NBLK
    right_block = grp * NB + NB - 1

    def edge_copy(off, c):
        return pltpu.make_async_remote_copy(
            send.at[rows_at(off * NB + NB - 1, c, 1)],
            recv.at[rows_at(left_block if off < 4 else right_block, c, 1)],
            a_ssem.at[NB - 1 + c, off], a_rsem.at[NB - 1 + c, off],
            device_id=grp_peer(off), device_id_type=MESH,
        )

    def own_copy(h):
        return pltpu.make_async_copy(
            send.at[rows_at(h, 0, comps)], recv.at[rows_at(grp * NB + h, 0, comps)], own_sem.at[h]
        )

    def own_edge(c, side):
        return pltpu.make_async_copy(
            send.at[rows_at(side * 4 * NB + NB - 1, c, 1)],
            recv.at[rows_at(right_block if side else left_block, c, 1)],
            own_sem.at[NB - 1 + c * 2 + side],
        )

    def put(c, h, off, rows):
        for tile in range(tiles):
            at = pl.ds((off * NB + h) * blk_rows + c * comp_rows + tile * 2 * FPG, 2 * FPG)
            send[at, :] = rows[:, tile * 128 : (tile + 1) * 128]

    order = (4, 3, 5, 2, 6, 1, 7)
    edges = (3, 5, 2, 6, 1, 7)
    both = slice(0, 2 * HOP)
    unit = 2 * FPG

    for c in range(comps):
        convert(c, 0)
        out = transform(c, 0, slice(HOP, 2 * HOP))
        d_keep[c] = out[:half_rows]
        d_send[c] = out[half_rows:]
        convert(c, NB - 1)
        out = transform(c, NB - 1, slice(0, HOP))
        a_send[c] = out[unit : unit + half_rows]
        a_keep[c, :unit] = out[:unit]
        a_keep[c, unit:] = out[unit + half_rows :]

    for h in range(NB - 1):
        for c in range(comps):
            if h + 1 < NB - 1:
                convert(c, h + 1)
            out = transform(c, h, both)
            for off in range(GRP):
                put(c, h, off, out[off * unit : (off + 1) * unit])
        if h == 0:
            pl.semaphore_wait(barrier, 21)
            for c in range(comps):
                a_copy(c).start()
                d_copy(c).start()
        for off in order:
            block_copy(off, h).start()
        own_copy(h).start()

    for c in range(comps):
        a_copy(c).wait_recv()
        for off in range(4):
            put(c, NB - 1, off, d_keep[c, off * unit : (off + 1) * unit] + a_recv[c, off * unit : (off + 1) * unit])
        d_copy(c).wait_recv()
        for off, slot in ((4, 0), (5, 1), (6, 2), (7, 3)):
            mine = a_keep[c, slot * unit : (slot + 1) * unit]
            at = 3 if off == 4 else off - 5
            put(c, NB - 1, off, mine + d_recv[c, at * unit : (at + 1) * unit])
        for off in edges:
            edge_copy(off, c).start()
        own_edge(c, 0).start()
        own_edge(c, 1).start()

    wts_copy.wait()
    scale = jnp.sqrt(wts_ref[...].reshape(1, points) * norm)
    for h in range(NB - 1):
        own_copy(h).wait()
        for off in order:
            block_copy(off, h).wait_recv()

    def gather(c, row):
        starts = [c * comp_rows + tile * 2 * FPG + row for tile in range(tiles)]
        return jnp.concatenate(
            [recv[pl.ds(start, NBLK, stride=blk_rows), :] for start in starts], axis=1
        )

    def red_copy(off):
        return pltpu.make_async_remote_copy(
            gsend.at[(red + off) % RED], rrecv.at[red], r_ssem.at[off], r_rsem.at[off],
            device_id=red_peer(off), device_id_type=MESH,
        )

    lane16 = lax.broadcasted_iota(jnp.int32, (NBLK // 2, 128), 1)
    lane32 = lax.broadcasted_iota(jnp.int32, (NBLK, 128), 1)
    for c in range(comps):
        own_edge(c, 0).wait()
        own_edge(c, 1).wait()
        for off in edges:
            edge_copy(off, c).wait_recv()
        for f in range(FPG):
            high, low = split(jnp.concatenate([gather(c, f), gather(c, FPG + f)], axis=0) * scale)
            stack = jnp.concatenate([high, low], axis=0)
            zs[f, c] = stack
            prod = lax.dot_general(
                stack, stack, (((1,), (1,)), ((), ())), preferred_element_type=jnp.float32
            )
            whole = prod[: 2 * NBLK] + prod[2 * NBLK :]
            if c > 0:
                whole = gram[f] + whole
            if c < comps - 1:
                gram[f] = whole
                continue
            whole = whole + pltpu.roll(whole, 64, 1)
            low_rows = pltpu.roll(whole[NBLK:], 32, 1)
            joined = whole[:NBLK] + jnp.where((lane32 & 32) == 0, low_rows, -low_rows)
            gsend[f] = jnp.where(lane16 < 64, joined[: NBLK // 2], joined[NBLK // 2 :])

            @pl.when(red != f)
            def _():
                red_copy((f + RED - red) % RED).start()

    part = gsend[red]
    for off in range(1, RED):
        red_copy(off).wait_recv()
        part = part + rrecv[(red + RED - off) % RED]
    zpart[...] = part

    def z_copy(off):
        return pltpu.make_async_remote_copy(
            zpart, zrecv.at[z], z_ssem.at[off], z_rsem.at[off],
            device_id=z_peer(off), device_id_type=MESH,
        )

    for off in (4, 3, 5, 2, 6, 1, 7):
        z_copy(off).start()
    zrecv[z] = part
    for off in range(1, ZS):
        z_copy(off).wait_recv()
    total = zrecv[0]
    for i in range(1, ZS):
        total = total + zrecv[i]

    rows_g = jnp.concatenate([total, pltpu.roll(total, 64, 1)], axis=0)
    upper = jnp.where(lane32 < 32, rows_g, jnp.where(lane32 < 64, -rows_g, 0.0))
    lower = jnp.where(
        lane32 < 32,
        pltpu.roll(rows_g, 96, 1),
        jnp.where(lane32 < 64, pltpu.roll(rows_g, 32, 1), 0.0),
    )
    embed = jnp.concatenate([upper, lower], axis=0)
    w = embed
    for step in range(ITERS):
        basis, lengths = orthonormalize(w)
        if step < ITERS - 1:
            padded = jnp.concatenate([basis, jnp.zeros_like(basis)], axis=0)
            w = jnp.dot(
                embed, padded, precision=lax.Precision.HIGHEST, preferred_element_type=jnp.float32
            )
    scaled = basis * (1.0 / jnp.sqrt(NBLK * lengths))
    v_re, v_im = scaled[:NBLK], scaled[NBLK:]
    swapped = pltpu.roll(jnp.concatenate([v_im, v_re], axis=0), MODES, 1)
    lane64 = lax.broadcasted_iota(jnp.int32, scaled.shape, 1)
    factors = jnp.where(lane64 < MODES, jnp.concatenate([v_re, -v_im], axis=0), swapped)
    column = jnp.concatenate([factors, jnp.broadcast_to(lengths, scaled.shape)], axis=0)
    vsend[...] = jnp.transpose(column)[: 2 * MODES]

    def v_copy(off):
        return pltpu.make_async_remote_copy(
            vsend, vrecv.at[red], v_ssem.at[off], v_rsem.at[off],
            device_id=red_peer(off), device_id_type=MESH,
        )

    for off in range(1, RED):
        v_copy(off).start()
    vrecv[red] = vsend[...]
    for off in range(1, RED):
        v_copy(off).wait_recv()

    lane8 = lax.broadcasted_iota(jnp.int32, (2 * MODES, 128), 1)
    unscale = 1.0 / scale
    energies = jnp.zeros((2 * MODES, 128), jnp.float32)
    for f in range(FPG):
        v = vrecv[f]
        energies = jnp.where(
            lane8 == f, jnp.broadcast_to(v[:, 2 * NBLK : 2 * NBLK + 1], v.shape), energies
        )
        v_hi = v.astype(jnp.bfloat16).astype(jnp.float32)
        first = jnp.where(lane8 < 64, v_hi, pltpu.roll(v_hi, 64, 1))
        rest = jnp.where(lane8 < 64, v - v_hi, 0.0)
        factor = jnp.concatenate([first, rest], axis=0).astype(jnp.bfloat16)
        for c in range(comps):
            out = fdot(factor, zs[f, c])
            out = (out[: 2 * MODES] + out[2 * MODES :]) * unscale
            modes_ref[0, f, c] = out[:MODES]
            modes_ref[1, f, c] = out[MODES:]
    en_ref[...] = energies[:MODES, :FPG]

    for c in range(comps):
        a_copy(c).wait_send()
        d_copy(c).wait_send()
        for off in edges:
            edge_copy(off, c).wait_send()
    for off in order:
        for h in range(NB - 1):
            block_copy(off, h).wait_send()
        red_copy(off).wait_send()
        z_copy(off).wait_send()
        v_copy(off).wait_send()


def shards(snapshots, kept_bins, weights):
    comps, times, points = snapshots.shape
    norm = 1.0 / (comps * points * lax.axis_size("sp"))
    f32, bf16 = jnp.float32, jnp.bfloat16
    dma = pltpu.SemaphoreType.DMA
    half = pltpu.VMEM((comps, GRP * FPG, points), f32)
    spectra = pltpu.VMEM((NBLK * 2 * FPG * comps * points // 128, 128), f32)
    table = pltpu.VMEM((2 * FPG * GRP, L), bf16)
    small = pltpu.VMEM((RED, NBLK // 2, 128), f32)
    n_msg = NB - 1 + comps
    hbm = pl.BlockSpec(memory_space=pltpu.HBM)
    vmem = pl.BlockSpec(memory_space=pltpu.VMEM)
    modes, energies = pl.pallas_call(
        functools.partial(kernel, norm),
        out_shape=(
            jax.ShapeDtypeStruct((2, FPG, comps, MODES, points), f32),
            jax.ShapeDtypeStruct((MODES, FPG), f32),
        ),
        in_specs=[hbm, hbm, hbm],
        out_specs=(vmem, vmem),
        scratch_shapes=[
            pltpu.SMEM((GRP * FPG,), jnp.int32),
            pltpu.VMEM((points,), f32),
            pltpu.VMEM((comps, times, points), f32),
            pltpu.VMEM((comps, times, points), bf16),
            pltpu.VMEM((comps, times, points), bf16),
            table,
            table,
            spectra,
            spectra,
            half,
            half,
            half,
            half,
            half,
            half,
            pltpu.VMEM((FPG, 2 * NBLK, 128), f32),
            pltpu.VMEM((FPG, comps, 4 * NBLK, points), bf16),
            small,
            small,
            pltpu.VMEM((NBLK // 2, 128), f32),
            small,
            pltpu.VMEM((8, 128), f32),
            pltpu.VMEM((RED, 8, 128), f32),
            dma((NB, comps)),
            dma((2,)),
            dma((NB - 1 + 2 * comps,)),
            dma((2, comps)),
            dma((2, comps)),
            dma((n_msg, GRP)),
            dma((n_msg, GRP)),
            dma((RED,)),
            dma((RED,)),
            dma((ZS,)),
            dma((ZS,)),
            dma((RED,)),
            dma((RED,)),
        ],
        compiler_params=pltpu.CompilerParams(
            collective_id=0, has_side_effects=True, vmem_limit_bytes=48 << 20
        ),
    )(*[pltpu.with_memory_space_constraint(a, pltpu.HBM) for a in (kept_bins, weights, snapshots)])
    return (jnp.transpose(modes, (0, 1, 3, 2, 4)), jnp.transpose(energies))


def solution(mesh):
    in_specs = (P(None, "grp", "sp"), P(), P("sp"))
    out_specs = (P(None, "grp", None, None, "sp"), P("grp", None))
    return jax.shard_map(shards, mesh=mesh, in_specs=in_specs, out_specs=out_specs, check_vma=False)
```

```python
import functools
import math

import jax
import jax.numpy as jnp
from jax import lax
from jax.experimental import pallas as pl
from jax.experimental.pallas import tpu as pltpu
from jax.sharding import PartitionSpec as P

L = 512
HOP = 256
MODES = 4
ITERS = 3
GRP = 8
FPG = 8
STAGES = 2
FPS = 4
RED = 8
ZS = 8
CORES = 2
NB = 4
NBLK = GRP * NB
MESH = pl.DeviceIdType.MESH


def cos_sin(phase):
    quarter = (phase + 64) >> 7
    rest = (phase - (quarter << 7)).astype(jnp.float32) * (2.0 * math.pi / L)
    sq = rest * rest
    sin = rest * (1.0 + sq * (-1.0 / 6 + sq * (1.0 / 120 + sq * (-1.0 / 5040 + sq * (1.0 / 362880)))))
    cos = 1.0 + sq * (-0.5 + sq * (1.0 / 24 + sq * (-1.0 / 720 + sq * (1.0 / 40320 - sq * (1.0 / 3628800)))))
    quarter = quarter & 3
    odd = (quarter & 1) == 1
    cos_q = jnp.where(odd, sin, cos)
    sin_q = jnp.where(odd, cos, sin)
    cos_q = jnp.where((quarter == 1) | (quarter == 2), -cos_q, cos_q)
    sin_q = jnp.where(quarter >= 2, -sin_q, sin_q)
    return cos_q, sin_q


def split(x):
    high = x.astype(jnp.bfloat16)
    low = (x - high.astype(jnp.float32)).astype(jnp.bfloat16)
    return high, low


def fdot(a, b):
    return jnp.dot(a, b, preferred_element_type=jnp.float32)


def make_tables(first_group, bins_ref, tab_hi, tab_lo):
    shape = (2 * FPS, HOP)
    row = lax.broadcasted_iota(jnp.int32, shape, 0)
    time = lax.broadcasted_iota(jnp.int32, shape, 1)
    scale = 1.0 / math.sqrt(3.0 * L / 8.0)
    window = (0.5 - 0.5 * cos_sin(time)[0]) * scale
    second = scale - window
    for off in range(GRP):
        group = (first_group + off) % GRP
        waves = [], []
        for stage in range(STAGES):
            first = group * FPG + stage * FPS
            bins = jnp.full(shape, bins_ref[first], jnp.int32)
            for f in range(1, FPS):
                bins = jnp.where((row & (FPS - 1)) == f, bins_ref[first + f], bins)
            cos, sin = cos_sin((bins * time) & (L - 1))
            wave = jnp.where(row < FPS, cos, -sin)
            waves[0].append(wave * window)
            waves[1].append(wave * jnp.where((bins & 1) == 1, -second, second))
        for half in range(2):
            high, low = split(jnp.concatenate(waves[half], axis=0))
            rows = pl.ds(off * 2 * FPG, 2 * FPG)
            tab_hi[rows, half * HOP : (half + 1) * HOP] = high
            tab_lo[rows, half * HOP : (half + 1) * HOP] = low


def orthonormalize(w):
    lane = lax.broadcasted_iota(jnp.int32, w.shape, 1)
    lane_row = lax.broadcasted_iota(jnp.int32, (1, w.shape[1]), 1)
    w_re, w_im = w[:NBLK], w[NBLK:]
    left = w
    basis = jnp.zeros_like(w)
    lengths = jnp.ones((1, w.shape[1]), jnp.float32)
    for m in range(MODES):
        length = jnp.sqrt(jnp.sum(left * left, axis=0, keepdims=True) + 1e-06)
        unit = left / length
        basis = jnp.where(lane == m, unit, basis)
        lengths = jnp.where(lane_row == m, length, lengths)
        if m < MODES - 1:
            q = jnp.broadcast_to(unit[:, m : m + 1], w.shape)
            q_re, q_im = q[:NBLK], q[NBLK:]
            coef_re = jnp.sum(q_re * w_re + q_im * w_im, axis=0, keepdims=True)
            coef_im = jnp.sum(q_re * w_im - q_im * w_re, axis=0, keepdims=True)
            left = left - jnp.concatenate(
                [coef_re * q_re - coef_im * q_im, coef_re * q_im + coef_im * q_re], axis=0
            )
    return basis, lengths


def pack(whole, lane, row):
    whole = whole + pltpu.roll(whole, 64, 1)
    low_rows = pltpu.roll(whole[NBLK:], 32, 1)
    even = (lane & 32) == 0
    joined = whole[:NBLK] + jnp.where(even, low_rows, -low_rows)
    other = pltpu.roll(joined, 32, 1)
    tri = jnp.where((row <= (lane & 31)) == even, joined, other)
    tile = tri[:8]
    lane8 = lane[:8]
    for i in range(1, 4):
        tile = jnp.where(lane8 >= 32 * i, tri[8 * i : 8 * i + 8], tile)
    return tile


def unpack(tile, lane, row):
    tri = jnp.concatenate([tile] + [pltpu.roll(tile, 128 - 32 * i, 1) for i in range(1, 4)], axis=0)
    flipped = jnp.transpose(jnp.concatenate([tri, jnp.zeros((96, 128), jnp.float32)], axis=0))[:NBLK]
    g_re = jnp.where(row <= lane, tri, flipped)
    g_im = jnp.where(row > lane, tri, jnp.where(row < lane, -flipped, 0.0))
    right_re = jnp.where(lane < 64, pltpu.roll(g_re, 32, 1), 0.0)
    right_im = jnp.where(lane < 64, pltpu.roll(g_im, 32, 1), 0.0)
    upper = jnp.where(lane < 32, g_re, -right_im)
    lower = jnp.where(lane < 32, g_im, right_re)
    return jnp.concatenate([upper, lower], axis=0)


def subspace(embed):
    w = embed
    for step in range(ITERS):
        basis, lengths = orthonormalize(w)
        if step < ITERS - 1:
            padded = jnp.concatenate([basis, jnp.zeros_like(basis)], axis=0)
            w = jnp.dot(
                embed, padded, precision=lax.Precision.HIGHEST, preferred_element_type=jnp.float32
            )
    scaled = basis * (1.0 / jnp.sqrt(NBLK * lengths))
    v_re, v_im = scaled[:NBLK], scaled[NBLK:]
    swapped = pltpu.roll(jnp.concatenate([v_im, v_re], axis=0), MODES, 1)
    lane64 = lax.broadcasted_iota(jnp.int32, scaled.shape, 1)
    factors = jnp.where(lane64 < MODES, jnp.concatenate([v_re, -v_im], axis=0), swapped)
    column = jnp.concatenate([factors, jnp.broadcast_to(lengths, scaled.shape)], axis=0)
    return jnp.transpose(column)[: 2 * MODES]


def kernel(
    norm,
    bins_hbm,
    wts_hbm,
    snap_ref,
    modes_ref,
    en_ref,
    bins_ref,
    wts_ref,
    data,
    d_hi,
    d_lo,
    tab_hi,
    tab_lo,
    send,
    recv,
    a_send,
    d_send,
    a_keep,
    d_keep,
    a_recv,
    d_recv,
    zs,
    gsend,
    rrecv,
    zpart,
    zrecv,
    vsend,
    vrecv,
    in_sem,
    arg_sem,
    own_sem,
    h_ssem,
    h_rsem,
    a_ssem,
    a_rsem,
    e_ssem,
    e_rsem,
    r_ssem,
    r_rsem,
    z_ssem,
    z_rsem,
    v_ssem,
    v_rsem,
):
    comps = data.shape[0]
    points = data.shape[2]
    tiles = points // 128
    comp_rows = tiles * 2 * FPS
    blk_rows = comps * comp_rows
    half_rows = GRP * FPG
    grp = lax.axis_index("grp")
    sp = lax.axis_index("sp")
    core = sp % CORES
    z = (sp // CORES) % ZS
    x = sp // (CORES * ZS)
    red = x * CORES + core

    def grp_peer(off):
        return (grp + off) % GRP, sp

    def red_peer(off):
        other = (red + off) % RED
        return grp, ((other // CORES) * ZS + z) * CORES + other % CORES

    def z_peer(off):
        return grp, (x * ZS + (z + off) % ZS) * CORES + core

    bins_copy = pltpu.make_async_copy(bins_hbm, bins_ref, arg_sem.at[0])
    wts_copy = pltpu.make_async_copy(wts_hbm, wts_ref, arg_sem.at[1])
    bins_copy.start()
    barrier = pltpu.get_barrier_semaphore()
    for off in (4, 3, 5, 2, 6, 1, 7):
        pl.semaphore_signal(barrier, inc=1, device_id=grp_peer(off), device_id_type=MESH)

    def load(c, h):
        rows = pl.ds(h * HOP, HOP)
        return pltpu.make_async_copy(snap_ref.at[c, rows], data.at[c, rows], in_sem.at[h, c])

    for h in (0, NB - 1):
        for c in range(comps):
            load(c, h).start()
    for off in (4, 3, 5, 2, 6, 1, 7):
        for peer in (z_peer, red_peer):
            pl.semaphore_signal(barrier, inc=1, device_id=peer(off), device_id_type=MESH)
    for h in range(1, NB - 1):
        for c in range(comps):
            load(c, h).start()
    wts_copy.start()

    bins_copy.wait()
    make_tables(grp, bins_ref, tab_hi, tab_lo)

    def convert(c, h):
        load(c, h).wait()
        rows = pl.ds(h * HOP, HOP)
        high, low = split(data[c, rows])
        d_hi[c, rows] = high
        d_lo[c, rows] = low

    def transform(c, h_first, cols):
        rows = pl.ds(h_first * HOP, cols.stop - cols.start)
        high = d_hi[c, rows]
        t_hi = tab_hi[:, cols]
        return fdot(t_hi, high) + (fdot(tab_lo[:, cols], high) + fdot(t_hi, d_lo[c, rows]))

    a_copy = pltpu.make_async_remote_copy(
        a_send, a_recv, h_ssem.at[0], h_rsem.at[0], device_id=grp_peer(1), device_id_type=MESH
    )
    d_copy = pltpu.make_async_remote_copy(
        d_send, d_recv, h_ssem.at[1], h_rsem.at[1], device_id=grp_peer(GRP - 1), device_id_type=MESH
    )
    left_block = (grp * NB + NBLK - 1) % NBLK
    right_block = grp * NB + NB - 1

    def sent(stage, off, h):
        return pl.ds(((stage * GRP + off) * NB + h) * blk_rows, blk_rows)

    def landed(stage, block):
        return pl.ds(pl.multiple_of((stage * NBLK + block) * blk_rows, 8), blk_rows)

    def target(off, h):
        if h < NB - 1:
            return grp * NB + h
        return left_block if off < 4 else right_block

    def block_copy(stage, off, h):
        return pltpu.make_async_remote_copy(
            send.at[sent(stage, off, h)], recv.at[landed(stage, target(off, h))],
            a_ssem.at[stage * NB + h, off], a_rsem.at[stage * NB + h, off],
            device_id=grp_peer(off), device_id_type=MESH,
        )

    def edge_copy(off, c):
        rows = c * comp_rows
        return pltpu.make_async_remote_copy(
            send.at[pl.ds(((GRP + off) * NB + NB - 1) * blk_rows + rows, comp_rows)],
            recv.at[
                pl.ds(
                    pl.multiple_of((NBLK + target(off, NB - 1)) * blk_rows + rows, 8), comp_rows
                )
            ],
            e_ssem.at[c, off], e_rsem.at[c, off],
            device_id=grp_peer(off), device_id_type=MESH,
        )

    def own_copy(stage, h):
        off, h_from = (4, NB - 1) if h == NB else (0, h)
        return pltpu.make_async_copy(
            send.at[sent(stage, off, h_from)], recv.at[landed(stage, target(off, h_from))],
            own_sem.at[stage, h],
        )

    def put(c, h, off, rows):
        for stage in range(STAGES):
            for tile in range(tiles):
                start = ((stage * GRP + off) * NB + h) * blk_rows + c * comp_rows + tile * 2 * FPS
                send[pl.ds(start, 2 * FPS), :] = rows[
                    stage * 2 * FPS : (stage + 1) * 2 * FPS, tile * 128 : (tile + 1) * 128
                ]

    def offsets(h):
        return edges if h == NB - 1 else order

    def start_sends(stage, h):
        if stage == STAGES - 1 and h == NB - 1:
            for c in range(comps):
                for off in edges:
                    edge_copy(off, c).start()
        else:
            for off in offsets(h):
                block_copy(stage, off, h).start()
        own_copy(stage, h).start()
        if h == NB - 1:
            own_copy(stage, NB).start()

    order = (4, 3, 5, 2, 6, 1, 7)
    edges = (3, 5, 2, 6, 1, 7)
    both = slice(0, 2 * HOP)
    unit = 2 * FPG

    for c in range(comps):
        convert(c, 0)
        out = transform(c, 0, slice(HOP, 2 * HOP))
        d_keep[c] = out[:half_rows]
        d_send[c] = out[half_rows:]
        convert(c, NB - 1)
        out = transform(c, NB - 1, slice(0, HOP))
        a_send[c] = out[unit : unit + half_rows]
        a_keep[c, :unit] = out[:unit]
        a_keep[c, unit:] = out[unit + half_rows :]
    pl.semaphore_wait(barrier, 21)
    a_copy.start()
    d_copy.start()

    for h in range(NB - 1):
        for c in range(comps):
            if h + 1 < NB - 1:
                convert(c, h + 1)
            out = transform(c, h, both)
            for off in range(GRP):
                put(c, h, off, out[off * unit : (off + 1) * unit])
        start_sends(0, h)

    a_copy.wait_recv()
    d_copy.wait_recv()
    for c in range(comps):
        for off in range(4):
            rows = slice(off * unit, (off + 1) * unit)
            put(c, NB - 1, off, d_keep[c, rows] + a_recv[c, rows])
        for off, slot in ((4, 0), (5, 1), (6, 2), (7, 3)):
            mine = a_keep[c, slot * unit : (slot + 1) * unit]
            at = 3 if off == 4 else off - 5
            put(c, NB - 1, off, mine + d_recv[c, at * unit : (at + 1) * unit])
    start_sends(0, NB - 1)
    for h in range(NB):
        start_sends(1, h)

    wts_copy.wait()
    scale = jnp.sqrt(wts_ref[...].reshape(1, points) * norm)
    unscale = 1.0 / scale
    lane32 = lax.broadcasted_iota(jnp.int32, (NBLK, 128), 1)
    row32 = lax.broadcasted_iota(jnp.int32, (NBLK, 128), 0)
    lane8 = lax.broadcasted_iota(jnp.int32, (2 * MODES, 128), 1)

    def gather(stage, c, row):
        starts = [stage * NBLK * blk_rows + c * comp_rows + tile * 2 * FPS + row for tile in range(tiles)]
        return jnp.concatenate(
            [recv[pl.ds(start, NBLK, stride=blk_rows), :] for start in starts], axis=1
        )

    def red_copy(stage, off):
        pair = pl.ds(((core + off) % CORES) * 2, 2)
        return pltpu.make_async_remote_copy(
            gsend.at[stage, pair], rrecv.at[stage, red], r_ssem.at[stage, off], r_rsem.at[stage, off],
            device_id=red_peer(off), device_id_type=MESH,
        )

    def z_copy(stage, off):
        return pltpu.make_async_remote_copy(
            zpart.at[stage], zrecv.at[stage, z], z_ssem.at[stage, off], z_rsem.at[stage, off],
            device_id=z_peer(off), device_id_type=MESH,
        )

    def v_copy(stage):
        return pltpu.make_async_remote_copy(
            vsend.at[stage], vrecv.at[stage, core], v_ssem.at[stage], v_rsem.at[stage],
            device_id=(grp, sp + 1 - 2 * core), device_id_type=MESH,
        )

    def finish_sends():
        a_copy.wait_send()
        d_copy.wait_send()
        for stage in range(STAGES):
            for h in range(NB - 1 if stage == STAGES - 1 else NB):
                for off in offsets(h):
                    block_copy(stage, off, h).wait_send()
        for c in range(comps):
            for off in edges:
                edge_copy(off, c).wait_send()

    energies = jnp.zeros((2 * MODES, 128), jnp.float32)
    for stage in range(STAGES):
        last = stage == STAGES - 1
        for h in range(NB + 1):
            own_copy(stage, h).wait()
        for h in range(NB - 1 if last else NB):
            for off in offsets(h):
                block_copy(stage, off, h).wait_recv()

        whole = [None] * FPS
        for c in range(comps):
            if last:
                for off in edges:
                    edge_copy(off, c).wait_recv()
            for f in range(FPS):
                parts = [gather(stage, c, f), gather(stage, c, FPS + f)]
                high, low = split(jnp.concatenate(parts, axis=0) * scale)
                stack = jnp.concatenate([high, low], axis=0)
                zs[stage * FPS + f, c] = stack
                prod = lax.dot_general(
                    stack, stack, (((1,), (1,)), ((), ())), preferred_element_type=jnp.float32
                )
                half = prod[: 2 * NBLK] + prod[2 * NBLK :]
                whole[f] = half if c == 0 else whole[f] + half
        for f in range(FPS):
            gsend[stage, f] = pack(whole[f], lane32, row32)

        for off in (4, 3, 5, 2, 6, 1, 7):
            red_copy(stage, off).start()
        rrecv[stage, red] = gsend[stage, pl.ds(core * 2, 2)]
        if last:
            finish_sends()
        for off in range(1, RED):
            red_copy(stage, off).wait_recv()
        part = rrecv[stage, 0]
        for i in range(1, RED):
            part = part + rrecv[stage, i]
        zpart[stage] = part
        for off in (4, 3, 5, 2, 6, 1, 7):
            z_copy(stage, off).start()
        zrecv[stage, z] = part
        for off in range(1, RED):
            red_copy(stage, off).wait_send()
        for off in range(1, ZS):
            z_copy(stage, off).wait_recv()
        total = zrecv[stage, 0]
        for i in range(1, ZS):
            total = total + zrecv[stage, i]

        factors = jnp.stack([subspace(unpack(total[j], lane32, row32)) for j in range(2)])
        vsend[stage] = factors
        v_copy(stage).start()
        vrecv[stage, core] = factors
        for off in range(1, ZS):
            z_copy(stage, off).wait_send()

        for f in range(FPS):
            if f == 2:
                v_copy(stage).wait()
            worker = core if f < 2 else 1 - core
            v = vrecv[stage, worker, f % 2]
            bin_at = stage * FPS + worker * 2 + f % 2
            energies = jnp.where(
                lane8 == bin_at, jnp.broadcast_to(v[:, 2 * NBLK : 2 * NBLK + 1], v.shape), energies
            )
            v_hi = v.astype(jnp.bfloat16).astype(jnp.float32)
            first = jnp.where(lane8 < 64, v_hi, pltpu.roll(v_hi, 64, 1))
            rest = jnp.where(lane8 < 64, v - v_hi, 0.0)
            factor = jnp.concatenate([first, rest], axis=0).astype(jnp.bfloat16)
            for c in range(comps):
                out = fdot(factor, zs[bin_at, c])
                out = (out[: 2 * MODES] + out[2 * MODES :]) * unscale
                modes_ref[0, bin_at, c] = out[:MODES]
                modes_ref[1, bin_at, c] = out[MODES:]
    en_ref[...] = energies[:MODES, :FPG]


def shards(snapshots, kept_bins, weights):
    comps, times, points = snapshots.shape
    norm = 1.0 / (comps * points * lax.axis_size("sp"))
    f32, bf16 = jnp.float32, jnp.bfloat16
    dma = pltpu.SemaphoreType.DMA
    half = pltpu.VMEM((comps, GRP * FPG, points), f32)
    spectra = pltpu.VMEM((NBLK * 2 * FPG * comps * points // 128, 128), f32)
    table = pltpu.VMEM((2 * FPG * GRP, L), bf16)
    hbm = pl.BlockSpec(memory_space=pltpu.HBM)
    vmem = pl.BlockSpec(memory_space=pltpu.VMEM)
    modes, energies = pl.pallas_call(
        functools.partial(kernel, norm),
        out_shape=(
            jax.ShapeDtypeStruct((2, FPG, comps, MODES, points), f32),
            jax.ShapeDtypeStruct((MODES, FPG), f32),
        ),
        in_specs=[hbm, hbm, hbm],
        out_specs=(vmem, vmem),
        scratch_shapes=[
            pltpu.SMEM((GRP * FPG,), jnp.int32),
            pltpu.VMEM((points,), f32),
            pltpu.VMEM((comps, times, points), f32),
            pltpu.VMEM((comps, times, points), bf16),
            pltpu.VMEM((comps, times, points), bf16),
            table,
            table,
            spectra,
            spectra,
            half,
            half,
            half,
            half,
            half,
            half,
            pltpu.VMEM((FPG, comps, 4 * NBLK, points), bf16),
            pltpu.VMEM((STAGES, FPS, 8, 128), f32),
            pltpu.VMEM((STAGES, RED, 2, 8, 128), f32),
            pltpu.VMEM((STAGES, 2, 8, 128), f32),
            pltpu.VMEM((STAGES, ZS, 2, 8, 128), f32),
            pltpu.VMEM((STAGES, 2, 8, 128), f32),
            pltpu.VMEM((STAGES, CORES, 2, 8, 128), f32),
            dma((NB, comps)),
            dma((2,)),
            dma((STAGES, NB + 1)),
            dma((2,)),
            dma((2,)),
            dma((STAGES * NB, GRP)),
            dma((STAGES * NB, GRP)),
            dma((comps, GRP)),
            dma((comps, GRP)),
            dma((STAGES, RED)),
            dma((STAGES, RED)),
            dma((STAGES, ZS)),
            dma((STAGES, ZS)),
            dma((STAGES,)),
            dma((STAGES,)),
        ],
        compiler_params=pltpu.CompilerParams(
            collective_id=0, has_side_effects=True, vmem_limit_bytes=48 << 20
        ),
    )(*[pltpu.with_memory_space_constraint(a, pltpu.HBM) for a in (kept_bins, weights, snapshots)])
    return (jnp.transpose(modes, (0, 1, 3, 2, 4)), jnp.transpose(energies))


def solution(mesh):
    in_specs = (P(None, "grp", "sp"), P(), P("sp"))
    out_specs = (P(None, "grp", None, None, "sp"), P("grp", None))
    return jax.shard_map(shards, mesh=mesh, in_specs=in_specs, out_specs=out_specs, check_vma=False)
```

```python
import functools
import math

import jax
import jax.numpy as jnp
from jax import lax
from jax.experimental import pallas as pl
from jax.experimental.pallas import tpu as pltpu
from jax.sharding import PartitionSpec as P

L = 512
HOP = 256
MODES = 4
ITERS = 3
GRP = 8
FPG = 8
STAGES = 2
FPS = 4
RED = 8
ZS = 8
CORES = 2
NB = 4
NBLK = GRP * NB
MESH = pl.DeviceIdType.MESH


def cos_sin(phase):
    quarter = (phase + 64) >> 7
    rest = (phase - (quarter << 7)).astype(jnp.float32) * (2.0 * math.pi / L)
    sq = rest * rest
    sin = rest * (1.0 + sq * (-1.0 / 6 + sq * (1.0 / 120 + sq * (-1.0 / 5040 + sq * (1.0 / 362880)))))
    cos = 1.0 + sq * (-0.5 + sq * (1.0 / 24 + sq * (-1.0 / 720 + sq * (1.0 / 40320 - sq * (1.0 / 3628800)))))
    quarter = quarter & 3
    odd = (quarter & 1) == 1
    cos_q = jnp.where(odd, sin, cos)
    sin_q = jnp.where(odd, cos, sin)
    cos_q = jnp.where((quarter == 1) | (quarter == 2), -cos_q, cos_q)
    sin_q = jnp.where(quarter >= 2, -sin_q, sin_q)
    return cos_q, sin_q


def split(x):
    high = x.astype(jnp.bfloat16)
    low = (x - high.astype(jnp.float32)).astype(jnp.bfloat16)
    return high, low


def fdot(a, b):
    return jnp.dot(a, b, preferred_element_type=jnp.float32)


def make_tables(first_group, bins_ref, tab_hi, tab_lo):
    shape = (2 * FPS, HOP)
    row = lax.broadcasted_iota(jnp.int32, shape, 0)
    time = lax.broadcasted_iota(jnp.int32, shape, 1)
    scale = 1.0 / math.sqrt(3.0 * L / 8.0)
    window = (0.5 - 0.5 * cos_sin(time)[0]) * scale
    second = scale - window
    for off in range(GRP):
        group = (first_group + off) % GRP
        waves = [], []
        for stage in range(STAGES):
            first = group * FPG + stage * FPS
            bins = jnp.full(shape, bins_ref[first], jnp.int32)
            for f in range(1, FPS):
                bins = jnp.where((row & (FPS - 1)) == f, bins_ref[first + f], bins)
            cos, sin = cos_sin((bins * time) & (L - 1))
            wave = jnp.where(row < FPS, cos, -sin)
            waves[0].append(wave * window)
            waves[1].append(wave * jnp.where((bins & 1) == 1, -second, second))
        for half in range(2):
            high, low = split(jnp.concatenate(waves[half], axis=0))
            rows = pl.ds(off * 2 * FPG, 2 * FPG)
            tab_hi[rows, half * HOP : (half + 1) * HOP] = high
            tab_lo[rows, half * HOP : (half + 1) * HOP] = low


def orthonormalize(w):
    lane = lax.broadcasted_iota(jnp.int32, w.shape, 1)
    lane_row = lax.broadcasted_iota(jnp.int32, (1, w.shape[1]), 1)
    w_re, w_im = w[:NBLK], w[NBLK:]
    left = w
    basis = jnp.zeros_like(w)
    lengths = jnp.ones((1, w.shape[1]), jnp.float32)
    for m in range(MODES):
        length = jnp.sqrt(jnp.sum(left * left, axis=0, keepdims=True) + 1e-06)
        unit = left * (1.0 / length)
        basis = jnp.where(lane == m, unit, basis)
        lengths = jnp.where(lane_row == m, length, lengths)
        if m < MODES - 1:
            q = jnp.broadcast_to(unit[:, m : m + 1], w.shape)
            q_re, q_im = q[:NBLK], q[NBLK:]
            coef_re = jnp.sum(q_re * w_re + q_im * w_im, axis=0, keepdims=True)
            coef_im = jnp.sum(q_re * w_im - q_im * w_re, axis=0, keepdims=True)
            left = left - jnp.concatenate(
                [coef_re * q_re - coef_im * q_im, coef_re * q_im + coef_im * q_re], axis=0
            )
    return basis, lengths


def pack(whole, lane, row):
    whole = whole + pltpu.roll(whole, 64, 1)
    low_rows = pltpu.roll(whole[NBLK:], 32, 1)
    even = (lane & 32) == 0
    joined = whole[:NBLK] + jnp.where(even, low_rows, -low_rows)
    other = pltpu.roll(joined, 32, 1)
    tri = jnp.where((row <= (lane & 31)) == even, joined, other)
    tile = tri[:8]
    lane8 = lane[:8]
    for i in range(1, 4):
        tile = jnp.where(lane8 >= 32 * i, tri[8 * i : 8 * i + 8], tile)
    return tile


def unpack(tile, lane, row):
    tri = jnp.concatenate([tile] + [pltpu.roll(tile, 128 - 32 * i, 1) for i in range(1, 4)], axis=0)
    flipped = jnp.transpose(jnp.concatenate([tri, jnp.zeros((96, 128), jnp.float32)], axis=0))[:NBLK]
    g_re = jnp.where(row <= lane, tri, flipped)
    g_im = jnp.where(row > lane, tri, jnp.where(row < lane, -flipped, 0.0))
    right_re = jnp.where(lane < 64, pltpu.roll(g_re, 32, 1), 0.0)
    right_im = jnp.where(lane < 64, pltpu.roll(g_im, 32, 1), 0.0)
    upper = jnp.where(lane < 32, g_re, -right_im)
    lower = jnp.where(lane < 32, g_im, right_re)
    return jnp.concatenate([upper, lower], axis=0)


def subspace(embed):
    e_hi = embed.astype(jnp.bfloat16).astype(jnp.float32)
    e_both = e_hi + pltpu.roll(embed - e_hi, 64, 1)
    left = jnp.concatenate([e_both, e_hi], axis=1).astype(jnp.bfloat16)
    w = embed
    for step in range(ITERS):
        basis, lengths = orthonormalize(w)
        if step < ITERS - 1:
            high, low = split(basis)
            w = fdot(left, jnp.concatenate([high, high, low, jnp.zeros_like(low)], axis=0))
    scaled = basis * (1.0 / jnp.sqrt(NBLK * lengths))
    v_re, v_im = scaled[:NBLK], scaled[NBLK:]
    swapped = pltpu.roll(jnp.concatenate([v_im, v_re], axis=0), MODES, 1)
    lane64 = lax.broadcasted_iota(jnp.int32, scaled.shape, 1)
    factors = jnp.where(lane64 < MODES, jnp.concatenate([v_re, -v_im], axis=0), swapped)
    column = jnp.concatenate([factors, jnp.broadcast_to(lengths, scaled.shape)], axis=0)
    return jnp.transpose(column)[: 2 * MODES]


def kernel(
    norm,
    bins_hbm,
    wts_hbm,
    snap_ref,
    modes_ref,
    en_ref,
    bins_ref,
    wts_ref,
    data,
    d_hi,
    d_lo,
    tab_hi,
    tab_lo,
    send,
    recv,
    a_send,
    d_send,
    a_keep,
    d_keep,
    a_recv,
    d_recv,
    zs,
    gsend,
    rrecv,
    zpart,
    zrecv,
    vsend,
    vrecv,
    in_sem,
    arg_sem,
    own_sem,
    h_ssem,
    h_rsem,
    a_ssem,
    a_rsem,
    e_ssem,
    e_rsem,
    r_ssem,
    r_rsem,
    z_ssem,
    z_rsem,
    v_ssem,
    v_rsem,
):
    comps = data.shape[0]
    points = data.shape[2]
    tiles = points // 128
    comp_rows = tiles * 2 * FPS
    blk_rows = comps * comp_rows
    half_rows = GRP * FPG
    grp = lax.axis_index("grp")
    sp = lax.axis_index("sp")
    core = sp % CORES
    z = (sp // CORES) % ZS
    x = sp // (CORES * ZS)
    red = x * CORES + core

    def grp_peer(off):
        return (grp + off) % GRP, sp

    def red_peer(off):
        other = (red + off) % RED
        return grp, ((other // CORES) * ZS + z) * CORES + other % CORES

    def z_peer(off):
        return grp, (x * ZS + (z + off) % ZS) * CORES + core

    bins_copy = pltpu.make_async_copy(bins_hbm, bins_ref, arg_sem.at[0])
    wts_copy = pltpu.make_async_copy(wts_hbm, wts_ref, arg_sem.at[1])
    bins_copy.start()
    barrier = pltpu.get_barrier_semaphore()
    for off in (4, 3, 5, 2, 6, 1, 7):
        pl.semaphore_signal(barrier, inc=1, device_id=grp_peer(off), device_id_type=MESH)

    def load(c, h):
        rows = pl.ds(h * HOP, HOP)
        return pltpu.make_async_copy(snap_ref.at[c, rows], data.at[c, rows], in_sem.at[h, c])

    for h in (0, NB - 1):
        for c in range(comps):
            load(c, h).start()
    for off in (4, 3, 5, 2, 6, 1, 7):
        for peer in (z_peer, red_peer):
            pl.semaphore_signal(barrier, inc=1, device_id=peer(off), device_id_type=MESH)
    for h in range(1, NB - 1):
        for c in range(comps):
            load(c, h).start()
    wts_copy.start()

    bins_copy.wait()
    make_tables(grp, bins_ref, tab_hi, tab_lo)

    def convert(c, h):
        load(c, h).wait()
        rows = pl.ds(h * HOP, HOP)
        high, low = split(data[c, rows])
        d_hi[c, rows] = high
        d_lo[c, rows] = low

    def transform(c, h_first, cols):
        rows = pl.ds(h_first * HOP, cols.stop - cols.start)
        high = d_hi[c, rows]
        t_hi = tab_hi[:, cols]
        return fdot(t_hi, high) + (fdot(tab_lo[:, cols], high) + fdot(t_hi, d_lo[c, rows]))

    a_copy = pltpu.make_async_remote_copy(
        a_send, a_recv, h_ssem.at[0], h_rsem.at[0], device_id=grp_peer(1), device_id_type=MESH
    )
    d_copy = pltpu.make_async_remote_copy(
        d_send, d_recv, h_ssem.at[1], h_rsem.at[1], device_id=grp_peer(GRP - 1), device_id_type=MESH
    )
    left_block = (grp * NB + NBLK - 1) % NBLK
    right_block = grp * NB + NB - 1

    def sent(stage, off, h):
        return pl.ds(((stage * GRP + off) * NB + h) * blk_rows, blk_rows)

    def landed(stage, block):
        return pl.ds(pl.multiple_of((stage * NBLK + block) * blk_rows, 8), blk_rows)

    def target(off, h):
        if h < NB - 1:
            return grp * NB + h
        return left_block if off < 4 else right_block

    def block_copy(stage, off, h):
        return pltpu.make_async_remote_copy(
            send.at[sent(stage, off, h)], recv.at[landed(stage, target(off, h))],
            a_ssem.at[stage * NB + h, off], a_rsem.at[stage * NB + h, off],
            device_id=grp_peer(off), device_id_type=MESH,
        )

    def edge_copy(off, c):
        rows = c * comp_rows
        return pltpu.make_async_remote_copy(
            send.at[pl.ds(((GRP + off) * NB + NB - 1) * blk_rows + rows, comp_rows)],
            recv.at[
                pl.ds(
                    pl.multiple_of((NBLK + target(off, NB - 1)) * blk_rows + rows, 8), comp_rows
                )
            ],
            e_ssem.at[c, off], e_rsem.at[c, off],
            device_id=grp_peer(off), device_id_type=MESH,
        )

    def own_copy(stage, h):
        off, h_from = (4, NB - 1) if h == NB else (0, h)
        return pltpu.make_async_copy(
            send.at[sent(stage, off, h_from)], recv.at[landed(stage, target(off, h_from))],
            own_sem.at[stage, h],
        )

    def put(c, h, off, rows):
        for stage in range(STAGES):
            for tile in range(tiles):
                start = ((stage * GRP + off) * NB + h) * blk_rows + c * comp_rows + tile * 2 * FPS
                send[pl.ds(start, 2 * FPS), :] = rows[
                    stage * 2 * FPS : (stage + 1) * 2 * FPS, tile * 128 : (tile + 1) * 128
                ]

    def offsets(h):
        return edges if h == NB - 1 else order

    def start_sends(stage, h):
        if stage == STAGES - 1 and h == NB - 1:
            for c in range(comps):
                for off in edges:
                    edge_copy(off, c).start()
        else:
            for off in offsets(h):
                block_copy(stage, off, h).start()
        own_copy(stage, h).start()
        if h == NB - 1:
            own_copy(stage, NB).start()

    order = (4, 3, 5, 2, 6, 1, 7)
    edges = (3, 5, 2, 6, 1, 7)
    both = slice(0, 2 * HOP)
    unit = 2 * FPG

    for c in range(comps):
        convert(c, 0)
        out = transform(c, 0, slice(HOP, 2 * HOP))
        d_keep[c] = out[:half_rows]
        d_send[c] = out[half_rows:]
        convert(c, NB - 1)
        out = transform(c, NB - 1, slice(0, HOP))
        a_send[c] = out[unit : unit + half_rows]
        a_keep[c, :unit] = out[:unit]
        a_keep[c, unit:] = out[unit + half_rows :]
    pl.semaphore_wait(barrier, 21)
    a_copy.start()
    d_copy.start()

    for h in range(NB - 1):
        for c in range(comps):
            if h + 1 < NB - 1:
                convert(c, h + 1)
            out = transform(c, h, both)
            for off in range(GRP):
                put(c, h, off, out[off * unit : (off + 1) * unit])
        start_sends(0, h)

    a_copy.wait_recv()
    d_copy.wait_recv()
    for c in range(comps):
        for off in range(4):
            rows = slice(off * unit, (off + 1) * unit)
            put(c, NB - 1, off, d_keep[c, rows] + a_recv[c, rows])
        for off, slot in ((4, 0), (5, 1), (6, 2), (7, 3)):
            mine = a_keep[c, slot * unit : (slot + 1) * unit]
            at = 3 if off == 4 else off - 5
            put(c, NB - 1, off, mine + d_recv[c, at * unit : (at + 1) * unit])
    start_sends(0, NB - 1)
    for h in range(NB):
        start_sends(1, h)

    wts_copy.wait()
    scale = jnp.sqrt(wts_ref[...].reshape(1, points) * norm)
    unscale = 1.0 / scale
    lane32 = lax.broadcasted_iota(jnp.int32, (NBLK, 128), 1)
    row32 = lax.broadcasted_iota(jnp.int32, (NBLK, 128), 0)
    lane8 = lax.broadcasted_iota(jnp.int32, (2 * MODES, 128), 1)

    def gather(stage, c, row):
        starts = [stage * NBLK * blk_rows + c * comp_rows + tile * 2 * FPS + row for tile in range(tiles)]
        return jnp.concatenate(
            [recv[pl.ds(start, NBLK, stride=blk_rows), :] for start in starts], axis=1
        )

    def red_copy(stage, off):
        pair = pl.ds(((core + off) % CORES) * 2, 2)
        return pltpu.make_async_remote_copy(
            gsend.at[stage, pair], rrecv.at[stage, red], r_ssem.at[stage, off], r_rsem.at[stage, off],
            device_id=red_peer(off), device_id_type=MESH,
        )

    def z_copy(stage, off):
        return pltpu.make_async_remote_copy(
            zpart.at[stage], zrecv.at[stage, z], z_ssem.at[stage, off], z_rsem.at[stage, off],
            device_id=z_peer(off), device_id_type=MESH,
        )

    def v_copy(stage):
        return pltpu.make_async_remote_copy(
            vsend.at[stage], vrecv.at[stage, core], v_ssem.at[stage], v_rsem.at[stage],
            device_id=(grp, sp + 1 - 2 * core), device_id_type=MESH,
        )

    def finish_sends():
        a_copy.wait_send()
        d_copy.wait_send()
        for stage in range(STAGES):
            for h in range(NB - 1 if stage == STAGES - 1 else NB):
                for off in offsets(h):
                    block_copy(stage, off, h).wait_send()
        for c in range(comps):
            for off in edges:
                edge_copy(off, c).wait_send()

    energies = jnp.zeros((2 * MODES, 128), jnp.float32)
    for stage in range(STAGES):
        last = stage == STAGES - 1
        for h in range(NB + 1):
            own_copy(stage, h).wait()
        for h in range(NB - 1 if last else NB):
            for off in offsets(h):
                block_copy(stage, off, h).wait_recv()

        whole = [None] * FPS
        for c in range(comps):
            if last:
                for off in edges:
                    edge_copy(off, c).wait_recv()
            for f in range(FPS):
                parts = [gather(stage, c, f), gather(stage, c, FPS + f)]
                high, low = split(jnp.concatenate(parts, axis=0) * scale)
                stack = jnp.concatenate([high, low], axis=0)
                zs[stage * FPS + f, c] = stack
                prod = lax.dot_general(
                    stack, stack, (((1,), (1,)), ((), ())), preferred_element_type=jnp.float32
                )
                half = prod[: 2 * NBLK] + prod[2 * NBLK :]
                whole[f] = half if c == 0 else whole[f] + half
        for f in range(FPS):
            gsend[stage, f] = pack(whole[f], lane32, row32)

        for off in (4, 3, 5, 2, 6, 1, 7):
            red_copy(stage, off).start()
        rrecv[stage, red] = gsend[stage, pl.ds(core * 2, 2)]
        if last:
            finish_sends()
        for off in range(1, RED):
            red_copy(stage, off).wait_recv()
        part = rrecv[stage, 0]
        for i in range(1, RED):
            part = part + rrecv[stage, i]
        zpart[stage] = part
        for off in (4, 3, 5, 2, 6, 1, 7):
            z_copy(stage, off).start()
        zrecv[stage, z] = part
        for off in range(1, RED):
            red_copy(stage, off).wait_send()
        for off in range(1, ZS):
            z_copy(stage, off).wait_recv()
        total = zrecv[stage, 0]
        for i in range(1, ZS):
            total = total + zrecv[stage, i]

        factors = jnp.stack([subspace(unpack(total[j], lane32, row32)) for j in range(2)])
        vsend[stage] = factors
        v_copy(stage).start()
        vrecv[stage, core] = factors
        for off in range(1, ZS):
            z_copy(stage, off).wait_send()

        for f in range(FPS):
            if f == 2:
                v_copy(stage).wait()
            worker = core if f < 2 else 1 - core
            v = vrecv[stage, worker, f % 2]
            bin_at = stage * FPS + worker * 2 + f % 2
            energies = jnp.where(
                lane8 == bin_at, jnp.broadcast_to(v[:, 2 * NBLK : 2 * NBLK + 1], v.shape), energies
            )
            v_hi = v.astype(jnp.bfloat16).astype(jnp.float32)
            first = jnp.where(lane8 < 64, v_hi, pltpu.roll(v_hi, 64, 1))
            rest = jnp.where(lane8 < 64, v - v_hi, 0.0)
            factor = jnp.concatenate([first, rest], axis=0).astype(jnp.bfloat16)
            for c in range(comps):
                out = fdot(factor, zs[bin_at, c])
                out = (out[: 2 * MODES] + out[2 * MODES :]) * unscale
                modes_ref[0, bin_at, c] = out[:MODES]
                modes_ref[1, bin_at, c] = out[MODES:]
    en_ref[...] = energies[:MODES, :FPG]


def copy_out(modes_ref, en_ref, modes_out, en_out, sem):
    copies = [
        pltpu.make_async_copy(modes_ref, modes_out, sem.at[0]),
        pltpu.make_async_copy(en_ref, en_out, sem.at[1]),
    ]
    for copy in copies:
        copy.start()
    for copy in copies:
        copy.wait()


def shards(snapshots, kept_bins, weights):
    comps, times, points = snapshots.shape
    norm = 1.0 / (comps * points * lax.axis_size("sp"))
    f32, bf16 = jnp.float32, jnp.bfloat16
    dma = pltpu.SemaphoreType.DMA
    half = pltpu.VMEM((comps, GRP * FPG, points), f32)
    spectra = pltpu.VMEM((NBLK * 2 * FPG * comps * points // 128, 128), f32)
    table = pltpu.VMEM((2 * FPG * GRP, L), bf16)
    hbm = pl.BlockSpec(memory_space=pltpu.HBM)
    vmem = pl.BlockSpec(memory_space=pltpu.VMEM)
    modes, energies = pl.pallas_call(
        functools.partial(kernel, norm),
        out_shape=(
            jax.ShapeDtypeStruct((2, FPG, comps, MODES, points), f32),
            jax.ShapeDtypeStruct((MODES, FPG), f32),
        ),
        in_specs=[hbm, hbm, hbm],
        out_specs=(vmem, vmem),
        scratch_shapes=[
            pltpu.SMEM((GRP * FPG,), jnp.int32),
            pltpu.VMEM((points,), f32),
            pltpu.VMEM((comps, times, points), f32),
            pltpu.VMEM((comps, times, points), bf16),
            pltpu.VMEM((comps, times, points), bf16),
            table,
            table,
            spectra,
            spectra,
            half,
            half,
            half,
            half,
            half,
            half,
            pltpu.VMEM((FPG, comps, 4 * NBLK, points), bf16),
            pltpu.VMEM((STAGES, FPS, 8, 128), f32),
            pltpu.VMEM((STAGES, RED, 2, 8, 128), f32),
            pltpu.VMEM((STAGES, 2, 8, 128), f32),
            pltpu.VMEM((STAGES, ZS, 2, 8, 128), f32),
            pltpu.VMEM((STAGES, 2, 8, 128), f32),
            pltpu.VMEM((STAGES, CORES, 2, 8, 128), f32),
            dma((NB, comps)),
            dma((2,)),
            dma((STAGES, NB + 1)),
            dma((2,)),
            dma((2,)),
            dma((STAGES * NB, GRP)),
            dma((STAGES * NB, GRP)),
            dma((comps, GRP)),
            dma((comps, GRP)),
            dma((STAGES, RED)),
            dma((STAGES, RED)),
            dma((STAGES, ZS)),
            dma((STAGES, ZS)),
            dma((STAGES,)),
            dma((STAGES,)),
        ],
        compiler_params=pltpu.CompilerParams(
            collective_id=0, has_side_effects=True, vmem_limit_bytes=48 << 20
        ),
    )(*[pltpu.with_memory_space_constraint(a, pltpu.HBM) for a in (kept_bins, weights, snapshots)])
    modes, energies = pl.pallas_call(
        copy_out,
        out_shape=(
            jax.ShapeDtypeStruct((2, FPG, comps, MODES, points), f32),
            jax.ShapeDtypeStruct((MODES, FPG), f32),
        ),
        in_specs=[pl.BlockSpec(memory_space=pl.ANY)] * 2,
        out_specs=(hbm, hbm),
        scratch_shapes=[dma((2,))],
        compiler_params=pltpu.CompilerParams(vmem_limit_bytes=4 << 20),
    )(modes, energies)
    return (jnp.transpose(modes, (0, 1, 3, 2, 4)), jnp.transpose(energies))


def solution(mesh):
    in_specs = (P(None, "grp", "sp"), P(), P("sp"))
    out_specs = (P(None, "grp", None, None, "sp"), P("grp", None))
    return jax.shard_map(shards, mesh=mesh, in_specs=in_specs, out_specs=out_specs, check_vma=False)
```

```python
import functools
import math

import jax
import jax.numpy as jnp
from jax import lax
from jax.experimental import pallas as pl
from jax.experimental.pallas import tpu as pltpu
from jax.sharding import PartitionSpec as P

L = 512
HOP = 256
MODES = 4
ITERS = 3
GRP = 8
FPG = 8
STAGES = 2
FPS = 4
RED = 8
ZS = 8
CORES = 2
NB = 4
NBLK = GRP * NB
MESH = pl.DeviceIdType.MESH


def cos_sin(phase):
    quarter = (phase + 64) >> 7
    rest = (phase - (quarter << 7)).astype(jnp.float32) * (2.0 * math.pi / L)
    sq = rest * rest
    sin = rest * (1.0 + sq * (-1.0 / 6 + sq * (1.0 / 120 + sq * (-1.0 / 5040 + sq * (1.0 / 362880)))))
    cos = 1.0 + sq * (-0.5 + sq * (1.0 / 24 + sq * (-1.0 / 720 + sq * (1.0 / 40320 - sq * (1.0 / 3628800)))))
    quarter = quarter & 3
    odd = (quarter & 1) == 1
    cos_q = jnp.where(odd, sin, cos)
    sin_q = jnp.where(odd, cos, sin)
    cos_q = jnp.where((quarter == 1) | (quarter == 2), -cos_q, cos_q)
    sin_q = jnp.where(quarter >= 2, -sin_q, sin_q)
    return cos_q, sin_q


def split(x):
    high = x.astype(jnp.bfloat16)
    low = (x - high.astype(jnp.float32)).astype(jnp.bfloat16)
    return high, low


def fdot(a, b):
    return jnp.dot(a, b, preferred_element_type=jnp.float32)


def make_tables(first_group, bins_ref, tab_hi, tab_lo):
    shape = (2 * FPS, HOP)
    row = lax.broadcasted_iota(jnp.int32, shape, 0)
    time = lax.broadcasted_iota(jnp.int32, shape, 1)
    scale = 1.0 / math.sqrt(3.0 * L / 8.0)
    window = (0.5 - 0.5 * cos_sin(time)[0]) * scale
    second = scale - window
    for off in range(GRP):
        group = (first_group + off) % GRP
        waves = [], []
        for stage in range(STAGES):
            first = group * FPG + stage * FPS
            bins = jnp.full(shape, bins_ref[first], jnp.int32)
            for f in range(1, FPS):
                bins = jnp.where((row & (FPS - 1)) == f, bins_ref[first + f], bins)
            cos, sin = cos_sin((bins * time) & (L - 1))
            wave = jnp.where(row < FPS, cos, -sin)
            waves[0].append(wave * window)
            waves[1].append(wave * jnp.where((bins & 1) == 1, -second, second))
        for half in range(2):
            high, low = split(jnp.concatenate(waves[half], axis=0))
            rows = pl.ds(off * 2 * FPG, 2 * FPG)
            tab_hi[rows, half * HOP : (half + 1) * HOP] = high
            tab_lo[rows, half * HOP : (half + 1) * HOP] = low


def orthonormalize(w):
    lane = lax.broadcasted_iota(jnp.int32, w.shape, 1)
    lane_row = lax.broadcasted_iota(jnp.int32, (1, w.shape[1]), 1)
    w_re, w_im = w[:NBLK], w[NBLK:]
    left = w
    basis = jnp.zeros_like(w)
    lengths = jnp.ones((1, w.shape[1]), jnp.float32)
    for m in range(MODES):
        square = jnp.sum(left * left, axis=0, keepdims=True) + 1e-06
        inverse = lax.rsqrt(square)
        length = square * inverse
        unit = left * inverse
        basis = jnp.where(lane == m, unit, basis)
        lengths = jnp.where(lane_row == m, length, lengths)
        if m < MODES - 1:
            q = jnp.broadcast_to(unit[:, m : m + 1], w.shape)
            q_re, q_im = q[:NBLK], q[NBLK:]
            coef_re = jnp.sum(q_re * w_re + q_im * w_im, axis=0, keepdims=True)
            coef_im = jnp.sum(q_re * w_im - q_im * w_re, axis=0, keepdims=True)
            left = left - jnp.concatenate(
                [coef_re * q_re - coef_im * q_im, coef_re * q_im + coef_im * q_re], axis=0
            )
    return basis, lengths


def pack(whole, lane, row):
    whole = whole + pltpu.roll(whole, 64, 1)
    low_rows = pltpu.roll(whole[NBLK:], 32, 1)
    even = (lane & 32) == 0
    joined = whole[:NBLK] + jnp.where(even, low_rows, -low_rows)
    other = pltpu.roll(joined, 32, 1)
    tri = jnp.where((row <= (lane & 31)) == even, joined, other)
    tile = tri[:8]
    lane8 = lane[:8]
    for i in range(1, 4):
        tile = jnp.where(lane8 >= 32 * i, tri[8 * i : 8 * i + 8], tile)
    return tile


def unpack(tile, lane, row):
    tri = jnp.concatenate([tile] + [pltpu.roll(tile, 128 - 32 * i, 1) for i in range(1, 4)], axis=0)
    flipped = jnp.transpose(jnp.concatenate([tri, jnp.zeros((96, 128), jnp.float32)], axis=0))[:NBLK]
    g_re = jnp.where(row <= lane, tri, flipped)
    g_im = jnp.where(row > lane, tri, jnp.where(row < lane, -flipped, 0.0))
    right_re = jnp.where(lane < 64, pltpu.roll(g_re, 32, 1), 0.0)
    right_im = jnp.where(lane < 64, pltpu.roll(g_im, 32, 1), 0.0)
    upper = jnp.where(lane < 32, g_re, -right_im)
    lower = jnp.where(lane < 32, g_im, right_re)
    return jnp.concatenate([upper, lower], axis=0)


def subspace(embed):
    e_hi = embed.astype(jnp.bfloat16).astype(jnp.float32)
    e_both = e_hi + pltpu.roll(embed - e_hi, 64, 1)
    left = jnp.concatenate([e_both, e_hi], axis=1).astype(jnp.bfloat16)
    w = embed
    for step in range(ITERS):
        basis, lengths = orthonormalize(w)
        if step < ITERS - 1:
            high, low = split(basis)
            w = fdot(left, jnp.concatenate([high, high, low, jnp.zeros_like(low)], axis=0))
    scaled = basis * (1.0 / jnp.sqrt(NBLK * lengths))
    v_re, v_im = scaled[:NBLK], scaled[NBLK:]
    swapped = pltpu.roll(jnp.concatenate([v_im, v_re], axis=0), MODES, 1)
    lane64 = lax.broadcasted_iota(jnp.int32, scaled.shape, 1)
    factors = jnp.where(lane64 < MODES, jnp.concatenate([v_re, -v_im], axis=0), swapped)
    column = jnp.concatenate([factors, jnp.broadcast_to(lengths, scaled.shape)], axis=0)
    return jnp.transpose(column)[: 2 * MODES]


def kernel(
    norm,
    bins_hbm,
    wts_hbm,
    snap_ref,
    modes_ref,
    en_ref,
    bins_ref,
    wts_ref,
    data,
    d_hi,
    d_lo,
    tab_hi,
    tab_lo,
    send,
    recv,
    a_send,
    d_send,
    a_keep,
    d_keep,
    a_recv,
    d_recv,
    zs,
    gsend,
    rrecv,
    zpart,
    zrecv,
    vsend,
    vrecv,
    in_sem,
    arg_sem,
    own_sem,
    h_ssem,
    h_rsem,
    a_ssem,
    a_rsem,
    e_ssem,
    e_rsem,
    r_ssem,
    r_rsem,
    z_ssem,
    z_rsem,
    v_ssem,
    v_rsem,
):
    comps = data.shape[0]
    points = data.shape[2]
    tiles = points // 128
    comp_rows = tiles * 2 * FPS
    blk_rows = comps * comp_rows
    half_rows = GRP * FPG
    grp = lax.axis_index("grp")
    sp = lax.axis_index("sp")
    core = sp % CORES
    z = (sp // CORES) % ZS
    x = sp // (CORES * ZS)
    red = x * CORES + core

    def grp_peer(off):
        return (grp + off) % GRP, sp

    def red_peer(off):
        other = (red + off) % RED
        return grp, ((other // CORES) * ZS + z) * CORES + other % CORES

    def z_peer(off):
        return grp, (x * ZS + (z + off) % ZS) * CORES + core

    bins_copy = pltpu.make_async_copy(bins_hbm, bins_ref, arg_sem.at[0])
    wts_copy = pltpu.make_async_copy(wts_hbm, wts_ref, arg_sem.at[1])
    bins_copy.start()
    barrier = pltpu.get_barrier_semaphore()
    for off in (4, 3, 5, 2, 6, 1, 7):
        pl.semaphore_signal(barrier, inc=1, device_id=grp_peer(off), device_id_type=MESH)

    def load(c, h):
        rows = pl.ds(h * HOP, HOP)
        return pltpu.make_async_copy(snap_ref.at[c, rows], data.at[c, rows], in_sem.at[h, c])

    for h in (0, NB - 1):
        for c in range(comps):
            load(c, h).start()
    for off in (4, 3, 5, 2, 6, 1, 7):
        for peer in (z_peer, red_peer):
            pl.semaphore_signal(barrier, inc=1, device_id=peer(off), device_id_type=MESH)
    for h in range(1, NB - 1):
        for c in range(comps):
            load(c, h).start()
    wts_copy.start()

    bins_copy.wait()
    make_tables(grp, bins_ref, tab_hi, tab_lo)

    def convert(c, h):
        load(c, h).wait()
        rows = pl.ds(h * HOP, HOP)
        high, low = split(data[c, rows])
        d_hi[c, rows] = high
        d_lo[c, rows] = low

    def transform(c, h_first, cols):
        rows = pl.ds(h_first * HOP, cols.stop - cols.start)
        high = d_hi[c, rows]
        t_hi = tab_hi[:, cols]
        return fdot(t_hi, high) + (fdot(tab_lo[:, cols], high) + fdot(t_hi, d_lo[c, rows]))

    a_copy = pltpu.make_async_remote_copy(
        a_send, a_recv, h_ssem.at[0], h_rsem.at[0], device_id=grp_peer(1), device_id_type=MESH
    )
    d_copy = pltpu.make_async_remote_copy(
        d_send, d_recv, h_ssem.at[1], h_rsem.at[1], device_id=grp_peer(GRP - 1), device_id_type=MESH
    )
    left_block = (grp * NB + NBLK - 1) % NBLK
    right_block = grp * NB + NB - 1

    def sent(stage, off, h):
        return pl.ds(((stage * GRP + off) * NB + h) * blk_rows, blk_rows)

    def landed(stage, block):
        return pl.ds(pl.multiple_of((stage * NBLK + block) * blk_rows, 8), blk_rows)

    def target(off, h):
        if h < NB - 1:
            return grp * NB + h
        return left_block if off < 4 else right_block

    def block_copy(stage, off, h):
        return pltpu.make_async_remote_copy(
            send.at[sent(stage, off, h)], recv.at[landed(stage, target(off, h))],
            a_ssem.at[stage * NB + h, off], a_rsem.at[stage * NB + h, off],
            device_id=grp_peer(off), device_id_type=MESH,
        )

    def edge_copy(off, c):
        rows = c * comp_rows
        return pltpu.make_async_remote_copy(
            send.at[pl.ds(((GRP + off) * NB + NB - 1) * blk_rows + rows, comp_rows)],
            recv.at[
                pl.ds(
                    pl.multiple_of((NBLK + target(off, NB - 1)) * blk_rows + rows, 8), comp_rows
                )
            ],
            e_ssem.at[c, off], e_rsem.at[c, off],
            device_id=grp_peer(off), device_id_type=MESH,
        )

    def own_copy(stage, h):
        off, h_from = (4, NB - 1) if h == NB else (0, h)
        return pltpu.make_async_copy(
            send.at[sent(stage, off, h_from)], recv.at[landed(stage, target(off, h_from))],
            own_sem.at[stage, h],
        )

    def put(c, h, off, rows):
        for stage in range(STAGES):
            for tile in range(tiles):
                start = ((stage * GRP + off) * NB + h) * blk_rows + c * comp_rows + tile * 2 * FPS
                send[pl.ds(start, 2 * FPS), :] = rows[
                    stage * 2 * FPS : (stage + 1) * 2 * FPS, tile * 128 : (tile + 1) * 128
                ]

    def offsets(h):
        return edges if h == NB - 1 else order

    def start_sends(stage, h):
        if stage == STAGES - 1 and h == NB - 1:
            for c in range(comps):
                for off in edges:
                    edge_copy(off, c).start()
        else:
            for off in offsets(h):
                block_copy(stage, off, h).start()
        own_copy(stage, h).start()
        if h == NB - 1:
            own_copy(stage, NB).start()

    order = (4, 3, 5, 2, 6, 1, 7)
    edges = (3, 5, 2, 6, 1, 7)
    both = slice(0, 2 * HOP)
    unit = 2 * FPG

    for c in range(comps):
        convert(c, 0)
        out = transform(c, 0, slice(HOP, 2 * HOP))
        d_keep[c] = out[:half_rows]
        d_send[c] = out[half_rows:]
        convert(c, NB - 1)
        out = transform(c, NB - 1, slice(0, HOP))
        a_send[c] = out[unit : unit + half_rows]
        a_keep[c, :unit] = out[:unit]
        a_keep[c, unit:] = out[unit + half_rows :]
    pl.semaphore_wait(barrier, 21)
    a_copy.start()
    d_copy.start()

    for h in range(NB - 1):
        for c in range(comps):
            if h + 1 < NB - 1:
                convert(c, h + 1)
            out = transform(c, h, both)
            for off in range(GRP):
                put(c, h, off, out[off * unit : (off + 1) * unit])
        start_sends(0, h)

    a_copy.wait_recv()
    d_copy.wait_recv()
    for c in range(comps):
        for off in range(4):
            rows = slice(off * unit, (off + 1) * unit)
            put(c, NB - 1, off, d_keep[c, rows] + a_recv[c, rows])
        for off, slot in ((4, 0), (5, 1), (6, 2), (7, 3)):
            mine = a_keep[c, slot * unit : (slot + 1) * unit]
            at = 3 if off == 4 else off - 5
            put(c, NB - 1, off, mine + d_recv[c, at * unit : (at + 1) * unit])
    start_sends(0, NB - 1)
    for h in range(NB):
        start_sends(1, h)

    wts_copy.wait()
    scale = jnp.sqrt(wts_ref[...].reshape(1, points) * norm)
    unscale = 1.0 / scale
    lane32 = lax.broadcasted_iota(jnp.int32, (NBLK, 128), 1)
    row32 = lax.broadcasted_iota(jnp.int32, (NBLK, 128), 0)
    lane8 = lax.broadcasted_iota(jnp.int32, (2 * MODES, 128), 1)

    def gather(stage, c, row):
        starts = [stage * NBLK * blk_rows + c * comp_rows + tile * 2 * FPS + row for tile in range(tiles)]
        return jnp.concatenate(
            [recv[pl.ds(start, NBLK, stride=blk_rows), :] for start in starts], axis=1
        )

    def red_copy(stage, off):
        pair = pl.ds(((core + off) % CORES) * 2, 2)
        return pltpu.make_async_remote_copy(
            gsend.at[stage, pair], rrecv.at[stage, red], r_ssem.at[stage, off], r_rsem.at[stage, off],
            device_id=red_peer(off), device_id_type=MESH,
        )

    def z_copy(stage, off):
        return pltpu.make_async_remote_copy(
            zpart.at[stage], zrecv.at[stage, z], z_ssem.at[stage, off], z_rsem.at[stage, off],
            device_id=z_peer(off), device_id_type=MESH,
        )

    def v_copy(stage):
        return pltpu.make_async_remote_copy(
            vsend.at[stage], vrecv.at[stage, core], v_ssem.at[stage], v_rsem.at[stage],
            device_id=(grp, sp + 1 - 2 * core), device_id_type=MESH,
        )

    def finish_sends():
        a_copy.wait_send()
        d_copy.wait_send()
        for stage in range(STAGES):
            for h in range(NB - 1 if stage == STAGES - 1 else NB):
                for off in offsets(h):
                    block_copy(stage, off, h).wait_send()
        for c in range(comps):
            for off in edges:
                edge_copy(off, c).wait_send()

    energies = jnp.zeros((2 * MODES, 128), jnp.float32)
    for stage in range(STAGES):
        last = stage == STAGES - 1
        for h in range(NB + 1):
            own_copy(stage, h).wait()
        for h in range(NB - 1 if last else NB):
            for off in offsets(h):
                block_copy(stage, off, h).wait_recv()

        whole = [None] * FPS
        for c in range(comps):
            if last:
                for off in edges:
                    edge_copy(off, c).wait_recv()
            for f in range(FPS):
                parts = [gather(stage, c, f), gather(stage, c, FPS + f)]
                high, low = split(jnp.concatenate(parts, axis=0) * scale)
                stack = jnp.concatenate([high, low], axis=0)
                zs[stage * FPS + f, c] = stack
                prod = lax.dot_general(
                    stack, stack, (((1,), (1,)), ((), ())), preferred_element_type=jnp.float32
                )
                half = prod[: 2 * NBLK] + prod[2 * NBLK :]
                whole[f] = half if c == 0 else whole[f] + half
        for f in range(FPS):
            gsend[stage, f] = pack(whole[f], lane32, row32)

        for off in (4, 3, 5, 2, 6, 1, 7):
            red_copy(stage, off).start()
        rrecv[stage, red] = gsend[stage, pl.ds(core * 2, 2)]
        if last:
            finish_sends()
        for off in range(1, RED):
            red_copy(stage, off).wait_recv()
        part = rrecv[stage, 0]
        for i in range(1, RED):
            part = part + rrecv[stage, i]
        zpart[stage] = part
        for off in (4, 3, 5, 2, 6, 1, 7):
            z_copy(stage, off).start()
        zrecv[stage, z] = part
        for off in range(1, RED):
            red_copy(stage, off).wait_send()
        for off in range(1, ZS):
            z_copy(stage, off).wait_recv()
        total = zrecv[stage, 0]
        for i in range(1, ZS):
            total = total + zrecv[stage, i]

        factors = jnp.stack([subspace(unpack(total[j], lane32, row32)) for j in range(2)])
        vsend[stage] = factors
        v_copy(stage).start()
        vrecv[stage, core] = factors
        for off in range(1, ZS):
            z_copy(stage, off).wait_send()

        for f in range(FPS):
            if f == 2:
                v_copy(stage).wait()
            worker = core if f < 2 else 1 - core
            v = vrecv[stage, worker, f % 2]
            bin_at = stage * FPS + worker * 2 + f % 2
            energies = jnp.where(
                lane8 == bin_at, jnp.broadcast_to(v[:, 2 * NBLK : 2 * NBLK + 1], v.shape), energies
            )
            v_hi = v.astype(jnp.bfloat16).astype(jnp.float32)
            first = jnp.where(lane8 < 64, v_hi, pltpu.roll(v_hi, 64, 1))
            rest = jnp.where(lane8 < 64, v - v_hi, 0.0)
            factor = jnp.concatenate([first, rest], axis=0).astype(jnp.bfloat16)
            for c in range(comps):
                out = fdot(factor, zs[bin_at, c])
                out = (out[: 2 * MODES] + out[2 * MODES :]) * unscale
                modes_ref[0, bin_at, c] = out[:MODES]
                modes_ref[1, bin_at, c] = out[MODES:]
    en_ref[...] = energies[:MODES, :FPG]


def copy_out(modes_ref, en_ref, modes_out, en_out, sem):
    copies = [
        pltpu.make_async_copy(modes_ref, modes_out, sem.at[0]),
        pltpu.make_async_copy(en_ref, en_out, sem.at[1]),
    ]
    for copy in copies:
        copy.start()
    for copy in copies:
        copy.wait()


def shards(snapshots, kept_bins, weights):
    comps, times, points = snapshots.shape
    norm = 1.0 / (comps * points * lax.axis_size("sp"))
    f32, bf16 = jnp.float32, jnp.bfloat16
    dma = pltpu.SemaphoreType.DMA
    half = pltpu.VMEM((comps, GRP * FPG, points), f32)
    spectra = pltpu.VMEM((NBLK * 2 * FPG * comps * points // 128, 128), f32)
    table = pltpu.VMEM((2 * FPG * GRP, L), bf16)
    hbm = pl.BlockSpec(memory_space=pltpu.HBM)
    vmem = pl.BlockSpec(memory_space=pltpu.VMEM)
    modes, energies = pl.pallas_call(
        functools.partial(kernel, norm),
        out_shape=(
            jax.ShapeDtypeStruct((2, FPG, comps, MODES, points), f32),
            jax.ShapeDtypeStruct((MODES, FPG), f32),
        ),
        in_specs=[hbm, hbm, hbm],
        out_specs=(vmem, vmem),
        scratch_shapes=[
            pltpu.SMEM((GRP * FPG,), jnp.int32),
            pltpu.VMEM((points,), f32),
            pltpu.VMEM((comps, times, points), f32),
            pltpu.VMEM((comps, times, points), bf16),
            pltpu.VMEM((comps, times, points), bf16),
            table,
            table,
            spectra,
            spectra,
            half,
            half,
            half,
            half,
            half,
            half,
            pltpu.VMEM((FPG, comps, 4 * NBLK, points), bf16),
            pltpu.VMEM((STAGES, FPS, 8, 128), f32),
            pltpu.VMEM((STAGES, RED, 2, 8, 128), f32),
            pltpu.VMEM((STAGES, 2, 8, 128), f32),
            pltpu.VMEM((STAGES, ZS, 2, 8, 128), f32),
            pltpu.VMEM((STAGES, 2, 8, 128), f32),
            pltpu.VMEM((STAGES, CORES, 2, 8, 128), f32),
            dma((NB, comps)),
            dma((2,)),
            dma((STAGES, NB + 1)),
            dma((2,)),
            dma((2,)),
            dma((STAGES * NB, GRP)),
            dma((STAGES * NB, GRP)),
            dma((comps, GRP)),
            dma((comps, GRP)),
            dma((STAGES, RED)),
            dma((STAGES, RED)),
            dma((STAGES, ZS)),
            dma((STAGES, ZS)),
            dma((STAGES,)),
            dma((STAGES,)),
        ],
        compiler_params=pltpu.CompilerParams(
            collective_id=0, has_side_effects=True, vmem_limit_bytes=48 << 20
        ),
    )(*[pltpu.with_memory_space_constraint(a, pltpu.HBM) for a in (kept_bins, weights, snapshots)])
    modes, energies = pl.pallas_call(
        copy_out,
        out_shape=(
            jax.ShapeDtypeStruct((2, FPG, comps, MODES, points), f32),
            jax.ShapeDtypeStruct((MODES, FPG), f32),
        ),
        in_specs=[pl.BlockSpec(memory_space=pl.ANY)] * 2,
        out_specs=(hbm, hbm),
        scratch_shapes=[dma((2,))],
        compiler_params=pltpu.CompilerParams(vmem_limit_bytes=4 << 20),
    )(modes, energies)
    return (jnp.transpose(modes, (0, 1, 3, 2, 4)), jnp.transpose(energies))


def solution(mesh):
    in_specs = (P(None, "grp", "sp"), P(), P("sp"))
    out_specs = (P(None, "grp", None, None, "sp"), P("grp", None))
    return jax.shard_map(shards, mesh=mesh, in_specs=in_specs, out_specs=out_specs, check_vma=False)
```
